32 devices in a mesh: dp: 4 (over x, core), ctx: 4 (over z), fsdp: 2 (over y).
Axes of the slice: x: 2, y: 2, z: 4, core: 2. Of those that a mesh axis runs over, the one named last changes fastest.
Arguments:
- hidden: bfloat16 [8, 512, 2048], P(('dp', 'fsdp'), 'ctx'), may hold values from -6 to 6
- cotangent: bfloat16 [8, 512, 2048], P(('dp', 'fsdp'), 'ctx'), may hold values from -6 to 6
- ln1_gain: bfloat16 [2048], P(('ctx', 'fsdp')), may hold values from 0.099609375 to 1.8984375
- ln1_bias: bfloat16 [2048], P(('ctx', 'fsdp')), may hold values from -3 to 3
- ln2_gain: bfloat16 [2048], P(('ctx', 'fsdp')), may hold values from 0.099609375 to 1.8984375
- ln2_bias: bfloat16 [2048], P(('ctx', 'fsdp')), may hold values from -3 to 3
- w_qkv: bfloat16 [2048, 6144], P(None, ('ctx', 'fsdp')), may hold values from -1.5 to 1.5
- b_qkv: bfloat16 [6144], P(('ctx', 'fsdp')), may hold values from -3 to 3
- w_out: bfloat16 [2048, 2048], P(None, ('ctx', 'fsdp')), may hold values from -0.75 to 0.75
- b_out: bfloat16 [2048], P(('ctx', 'fsdp')), may hold values from -3 to 3
- w_fc1: bfloat16 [2048, 8192], P(None, ('ctx', 'fsdp')), may hold values from -0.125 to 0.125
- b_fc1: bfloat16 [8192], P(('ctx', 'fsdp')), may hold values from -3 to 3
- w_fc2: bfloat16 [8192, 2048], P(None, ('ctx', 'fsdp')), may hold values from -0.0625 to 0.0625
- b_fc2: bfloat16 [2048], P(('ctx', 'fsdp')), may hold values from -3 to 3
Outputs:
- output: bfloat16 [8, 512, 2048], P(('dp', 'fsdp'), 'ctx')
- input_grad: bfloat16 [8, 512, 2048], P(('dp', 'fsdp'), 'ctx')
- ln1_gain_grad: float32 [2048], P(('ctx', 'fsdp'))
- ln1_bias_grad: float32 [2048], P(('ctx', 'fsdp'))
- ln2_gain_grad: float32 [2048], P(('ctx', 'fsdp'))
- ln2_bias_grad: float32 [2048], P(('ctx', 'fsdp'))
- w_qkv_grad: float32 [2048, 6144], P(None, ('ctx', 'fsdp'))
- b_qkv_grad: float32 [6144], P(('ctx', 'fsdp'))
- w_out_grad: float32 [2048, 2048], P(None, ('ctx', 'fsdp'))
- b_out_grad: float32 [2048], P(('ctx', 'fsdp'))
- w_fc1_grad: float32 [2048, 8192], P(None, ('ctx', 'fsdp'))
- b_fc1_grad: float32 [8192], P(('ctx', 'fsdp'))
- w_fc2_grad: float32 [8192, 2048], P(None, ('ctx', 'fsdp'))
- b_fc2_grad: float32 [2048], P(('ctx', 'fsdp'))
The draws below stay inside these ranges and needn't reach their ends.
All inputs are finite; a program needn't handle non-finite values.
Results may differ from the reference program's by a relative error of at most 0.0096.
Values may be sent and summed in bfloat16 or wider, within the bound.
No kernel may reach another device: no remote copies, remote signals or barrier semaphores. Data moves between devices by JAX's collectives and lax.ppermute only.
A program may use at most 384 MiB of HBM per device.

```python
import math
import jax
import jax.numpy as jnp
from jax import lax

D = 2048
HEADS = 8
HEAD = 256
ROT = 64
FF = 8192
SEQ_LEN = 512
SEQS = 8


def draw_w_qkv(key, part):
    rng_first = jax.random.fold_in(key, 11)
    spread = 1.0 / math.sqrt(D)
    matrix = jax.random.normal(rng_first, (D, 3 * D), jnp.float32) * spread
    return jnp.clip(matrix, -1.5, 1.5).astype(jnp.bfloat16)


def block_levels(own_key, extent, split, low, high):
    factor_of, own = 1.0, jax.random.fold_in(own_key, 6)
    for axis_at, blocks in split:
        heights = jnp.exp(jax.random.uniform(jax.random.fold_in(own, axis_at), (blocks,), jnp.float32, low / len(split), high / len(split)))
        factor_of = factor_of * jnp.repeat(heights, extent[axis_at] // blocks).reshape([-1 if axis == axis_at else 1 for axis in range(len(extent))])
    return factor_of


def normal_values(own_key, shape, scale, most, pieces=(), held_as=jnp.bfloat16):
    loudness = block_levels(own_key, shape, pieces, -0.22, 0.18) if pieces else 1.0
    result = jax.random.normal(own_key, shape, jnp.float32) * scale * loudness
    return jnp.minimum(jnp.maximum(result, -most), most).astype(held_as)


def setup_inputs(seed: int = 0) -> dict:
    keys = jax.random.split(jax.random.key(seed), 15)
    hidden = normal_values(keys[0], (SEQS, SEQ_LEN, D), 1.0, 6.0, ((0, 8), (1, 4)))
    cotangent = normal_values(keys[1], (SEQS, SEQ_LEN, D), 1.0, 6.0, ((0, 8), (1, 4)))
    ln1_gain = jnp.clip(1.0 + 0.18 * jax.random.normal(keys[2], (D,), jnp.float32), 0.099609375, 1.8984375).astype(jnp.bfloat16)
    ln1_bias = normal_values(keys[3], (D,), 0.3, 3.0, ((0, 8),))
    ln2_gain = jnp.clip(1.0 + 0.18 * jax.random.normal(keys[4], (D,), jnp.float32), 0.099609375, 1.8984375).astype(jnp.bfloat16)
    ln2_bias = normal_values(keys[5], (D,), 0.3, 3.0, ((0, 8),))
    w_qkv = draw_w_qkv(jax.random.fold_in(keys[14], 71), 0)
    b_qkv = normal_values(keys[7], (3 * D,), 0.3, 3.0, ((0, 8),))
    w_out = normal_values(keys[8], (D, D), (D // 32) ** -0.5, 0.75, ((1, 8),))
    b_out = normal_values(keys[9], (D,), 0.3, 3.0, ((0, 8),))
    w_fc1 = normal_values(keys[10], (D, FF), D ** -0.5, 0.125, ((1, 8),))
    b_fc1 = normal_values(keys[11], (FF,), 0.5, 3.0, ((0, 8),))
    w_fc2 = normal_values(keys[12], (FF, D), FF ** -0.5, 0.0625, ((1, 8),))
    b_fc2 = normal_values(keys[13], (D,), 0.3, 3.0, ((0, 8),))
    return dict(hidden=hidden, cotangent=cotangent, ln1_gain=ln1_gain, ln1_bias=ln1_bias, ln2_gain=ln2_gain, ln2_bias=ln2_bias, w_qkv=w_qkv, b_qkv=b_qkv, w_out=w_out, b_out=b_out, w_fc1=w_fc1, b_fc1=b_fc1, w_fc2=w_fc2, b_fc2=b_fc2)


EPSILON = 1e-05
SQRT_HALF = 0.7071067811865476
INV_ROOT_TWO_PI = 0.3989422804014327
MASKED = -1e+30

def widen(tensor):
    return lax.optimization_barrier(tensor).astype(jnp.float32)

def normalize(inputs):
    centre = lax.optimization_barrier(jnp.mean(inputs, axis=-1, keepdims=True))
    centred = inputs - centre
    variance = lax.optimization_barrier(jnp.mean(centred * centred, axis=-1, keepdims=True))
    inv_std = lax.rsqrt(variance + EPSILON)
    return (centred * inv_std, inv_std)

def norm_backward(upstream, normed, inv_std):
    first_mean = lax.optimization_barrier(jnp.mean(upstream, axis=-1, keepdims=True))
    second_mean = lax.optimization_barrier(jnp.mean(upstream * normed, axis=-1, keepdims=True))
    return inv_std * (upstream - first_mean - normed * second_mean)

def gelu_parts(preact):
    normal_cdf = 0.5 * (1.0 + lax.erf(preact * SQRT_HALF))
    normal_pdf = jnp.exp(-0.5 * preact * preact) * INV_ROOT_TWO_PI
    return (preact * normal_cdf, normal_cdf + preact * normal_pdf)

def rotary_tables(positions, rot_dims):
    half_dims = rot_dims // 2
    frequency = jnp.exp(jnp.arange(half_dims).astype(jnp.float32) * (-2.0 * math.log(10000.0) / rot_dims))
    angles = positions[:, None] * frequency[None, :]
    return (jnp.cos(angles)[:, None, :], jnp.sin(angles)[:, None, :])

def rotate(tensor, cosine, sine_table, rot_dims):
    half_dims = rot_dims // 2
    leading = tensor[..., :half_dims]
    trailing = tensor[..., half_dims:rot_dims]
    return jnp.concatenate([leading * cosine - trailing * sine_table, trailing * cosine + leading * sine_table, tensor[..., rot_dims:]], axis=-1)

def one_sequence(inputs, cotangent, params):
    gain_one, shift_one, gain_two, shift_two, w_qkv, b_qkv, w_out, b_out, w_fc1, b_fc1, w_fc2, b_fc2 = params
    length = inputs.shape[0]
    score_scale = HEAD ** (-0.5)
    inputs_f = inputs.astype(jnp.float32)
    normed, inv_std = normalize(inputs_f)
    attn_in = (normed * gain_one.astype(jnp.float32) + shift_one.astype(jnp.float32)).astype(jnp.bfloat16)
    mlp_in = (normed * gain_two.astype(jnp.float32) + shift_two.astype(jnp.float32)).astype(jnp.bfloat16)
    joined = jnp.dot(attn_in, w_qkv, preferred_element_type=jnp.float32) + b_qkv.astype(jnp.float32)
    joined = joined.reshape(length, 3, HEADS, HEAD)
    positions = jnp.arange(length).astype(jnp.float32)
    cosine, sine_table = rotary_tables(positions, ROT)
    queries = rotate(joined[:, 0], cosine, sine_table, ROT).astype(jnp.bfloat16)
    keys_all = rotate(joined[:, 1], cosine, sine_table, ROT).astype(jnp.bfloat16)
    values = joined[:, 2].astype(jnp.bfloat16)
    causal = (jnp.arange(length)[:, None] >= jnp.arange(length)[None, :])[None]
    scores = jnp.einsum('qhd,khd->hqk', widen(queries), widen(keys_all)) * score_scale
    scores = jnp.where(causal, scores, MASKED)
    row_top = lax.optimization_barrier(jnp.max(scores, axis=-1, keepdims=True))
    weights_exp = jnp.where(causal, jnp.exp(scores - row_top), 0.0)
    row_total = lax.optimization_barrier(jnp.sum(weights_exp, axis=-1, keepdims=True))
    log_total = row_top + jnp.log(row_total)
    mixed = jnp.einsum('hqk,khd->qhd', widen(weights_exp.astype(jnp.bfloat16)), widen(values))
    attended = (mixed / jnp.transpose(row_total, (1, 0, 2))).astype(jnp.bfloat16)
    attended_flat = attended.reshape(length, HEADS * HEAD)
    branch_attn = jnp.dot(attended_flat, w_out, preferred_element_type=jnp.float32) + b_out.astype(jnp.float32)
    preact = jnp.dot(mlp_in, w_fc1, preferred_element_type=jnp.float32) + b_fc1.astype(jnp.float32)
    activated, slope = gelu_parts(preact)
    act_bf = activated.astype(jnp.bfloat16)
    branch_mlp = jnp.dot(act_bf, w_fc2, preferred_element_type=jnp.float32) + b_fc2.astype(jnp.float32)
    output = (inputs_f + branch_attn + branch_mlp).astype(jnp.bfloat16)
    upstream = cotangent.astype(jnp.float32)
    bias_out_grad = lax.optimization_barrier(jnp.sum(upstream, axis=0))
    fc2_grad = jnp.dot(act_bf.T, cotangent, preferred_element_type=jnp.float32)
    d_act = jnp.dot(cotangent, w_fc2.T, preferred_element_type=jnp.float32)
    d_preact = d_act * slope
    fc1_bias_grad = lax.optimization_barrier(jnp.sum(d_preact, axis=0))
    d_preact_bf = d_preact.astype(jnp.bfloat16)
    fc1_grad = jnp.dot(mlp_in.T, d_preact_bf, preferred_element_type=jnp.float32)
    d_mlp_in = jnp.dot(d_preact_bf, w_fc1.T, preferred_element_type=jnp.float32)
    out_grad = jnp.dot(attended_flat.T, cotangent, preferred_element_type=jnp.float32)
    d_attended = jnp.dot(cotangent, w_out.T, preferred_element_type=jnp.float32).astype(jnp.bfloat16).reshape(length, HEADS, HEAD)
    row_dot = jnp.transpose(lax.optimization_barrier(jnp.sum(widen(d_attended) * widen(attended), axis=-1)), (1, 0))[:, :, None]
    probability = jnp.where(causal, jnp.exp(scores - log_total), 0.0)
    d_probability = jnp.einsum('qhd,khd->hqk', widen(d_attended), widen(values))
    d_scores = (probability * (d_probability - row_dot) * score_scale).astype(jnp.bfloat16)
    d_queries = jnp.einsum('hqk,khd->qhd', widen(d_scores), widen(keys_all))
    d_keys = jnp.einsum('hqk,qhd->khd', widen(d_scores), widen(queries))
    d_values = jnp.einsum('hqk,qhd->khd', widen(probability.astype(jnp.bfloat16)), widen(d_attended))
    d_queries = rotate(d_queries, cosine, -sine_table, ROT)
    d_keys = rotate(d_keys, cosine, -sine_table, ROT)
    d_joined = jnp.stack([d_queries, d_keys, d_values], axis=1).reshape(length, 3 * HEADS * HEAD)
    qkv_bias_grad = lax.optimization_barrier(jnp.sum(d_joined, axis=0))
    d_joined_bf = d_joined.astype(jnp.bfloat16)
    qkv_grad = jnp.dot(attn_in.T, d_joined_bf, preferred_element_type=jnp.float32)
    d_attn_in = jnp.dot(d_joined_bf, w_qkv.T, preferred_element_type=jnp.float32)
    merged = d_attn_in * gain_one.astype(jnp.float32) + d_mlp_in * gain_two.astype(jnp.float32)
    input_grad = (upstream + norm_backward(merged, normed, inv_std)).astype(jnp.bfloat16)
    grads = (lax.optimization_barrier(jnp.sum(d_attn_in * normed, axis=0)), lax.optimization_barrier(jnp.sum(d_attn_in, axis=0)), lax.optimization_barrier(jnp.sum(d_mlp_in * normed, axis=0)), lax.optimization_barrier(jnp.sum(d_mlp_in, axis=0)), qkv_grad, qkv_bias_grad, out_grad, bias_out_grad, fc1_grad, fc1_bias_grad, fc2_grad, bias_out_grad)
    return (output, input_grad, grads)

def reference(hidden, cotangent, ln1_gain, ln1_bias, ln2_gain, ln2_bias, w_qkv, b_qkv, w_out, b_out, w_fc1, b_fc1, w_fc2, b_fc2):
    params = (ln1_gain, ln1_bias, ln2_gain, ln2_bias, w_qkv, b_qkv, w_out, b_out, w_fc1, b_fc1, w_fc2, b_fc2)

    def advance(carried, paired):
        output, input_grad, grads = one_sequence(paired[0], paired[1], params)
        return (tuple((running + addend for running, addend in zip(carried, grads))), (output, input_grad))
    zero_grads = tuple((jnp.zeros(member.shape, jnp.float32) for member in params))
    totals, results = lax.scan(advance, zero_grads, (hidden, cotangent))
    return (results[0], results[1], totals[0], totals[1], totals[2], totals[3], totals[4], totals[5], totals[6], totals[7], totals[8], totals[9], totals[10], totals[11])
```

```python
import math

import jax
import jax.numpy as jnp
from jax import lax
from jax.sharding import Mesh
from jax.sharding import PartitionSpec as P

HEADS = 8
HEAD = 256
ROT = 64


EPSILON = 1e-05
SQRT_HALF = 0.7071067811865476
INV_ROOT_TWO_PI = 0.3989422804014327
MASKED = -1e30


def from_behind(value, axis, steps):
    count = lax.axis_size(axis)
    pairs = [(source, (source + steps) % count) for source in range(count)]
    return lax.ppermute(value, axis, pairs)


def shifted(block, axis, distance):
    devices = range(lax.axis_size(axis))
    route = [(i - distance, i) for i in devices if i - distance in devices]
    return lax.ppermute(block, axis, route)


def normalize(inputs):
    centre = jnp.mean(inputs, axis=-1, keepdims=True)
    centred = inputs - centre
    variance = jnp.mean(centred * centred, axis=-1, keepdims=True)
    inv_std = lax.rsqrt(variance + EPSILON)
    return (centred * inv_std, inv_std)


def norm_backward(upstream, normed, inv_std):
    first_mean = jnp.mean(upstream, axis=-1, keepdims=True)
    second_mean = jnp.mean(upstream * normed, axis=-1, keepdims=True)
    return inv_std * (upstream - first_mean - normed * second_mean)


def gelu_parts(preact):
    normal_cdf = 0.5 * (1.0 + lax.erf(preact * SQRT_HALF))
    normal_pdf = jnp.exp(-0.5 * preact * preact) * INV_ROOT_TWO_PI
    return (preact * normal_cdf, normal_cdf + preact * normal_pdf)


def rotary_tables(positions, rot_dims):
    half_dims = rot_dims // 2
    frequency = jnp.exp(
        jnp.arange(half_dims).astype(jnp.float32) * (-2.0 * math.log(10000.0) / rot_dims)
    )
    angles = positions[:, None] * frequency[None, :]
    return (jnp.cos(angles)[:, None, :], jnp.sin(angles)[:, None, :])


def rotate(tensor, cosine, sine_table, rot_dims):
    half_dims = rot_dims // 2
    leading = tensor[..., :half_dims]
    trailing = tensor[..., half_dims:rot_dims]
    return jnp.concatenate(
        [
            leading * cosine - trailing * sine_table,
            trailing * cosine + leading * sine_table,
            tensor[..., rot_dims:],
        ],
        axis=-1,
    )


def contract_rows(left, right):
    return lax.dot_general(
        left, right, (((0,), (0,)), ((), ())), preferred_element_type=jnp.float32
    )


def contract_cols(left, right):
    return lax.dot_general(
        left, right, (((1,), (1,)), ((), ())), preferred_element_type=jnp.float32
    )


def body(
    hidden,
    cotangent,
    ln1_gain,
    ln1_bias,
    ln2_gain,
    ln2_bias,
    w_qkv,
    b_qkv,
    w_out,
    b_out,
    w_fc1,
    b_fc1,
    w_fc2,
    b_fc2,
):
    inputs = hidden[0]
    upstream_bf = cotangent[0]
    row_count = inputs.shape[0]
    score_scale = HEAD ** (-0.5)
    cycle_size = lax.axis_size("ctx")
    cycle_place = lax.axis_index("ctx")
    attn_gathered = (
        lax.all_gather(ln1_gain, ("ctx", "fsdp"), axis=0, tiled=True),
        lax.all_gather(ln1_bias, ("ctx", "fsdp"), axis=0, tiled=True),
        lax.all_gather(w_qkv, ("ctx", "fsdp"), axis=1, tiled=True),
        lax.all_gather(b_qkv, ("ctx", "fsdp"), axis=0, tiled=True),
        lax.all_gather(w_out, ("ctx", "fsdp"), axis=1, tiled=True),
        lax.all_gather(b_out, ("ctx", "fsdp"), axis=0, tiled=True),
    )
    mlp_gathered = (
        lax.all_gather(ln2_gain, ("ctx", "fsdp"), axis=0, tiled=True),
        lax.all_gather(ln2_bias, ("ctx", "fsdp"), axis=0, tiled=True),
        lax.all_gather(w_fc1, ("ctx", "fsdp"), axis=1, tiled=True),
        lax.all_gather(b_fc1, ("ctx", "fsdp"), axis=0, tiled=True),
        lax.all_gather(w_fc2, ("ctx", "fsdp"), axis=1, tiled=True),
        lax.all_gather(b_fc2, ("ctx", "fsdp"), axis=0, tiled=True),
    )
    gain_one, shift_one, full_qkv, full_bqkv, full_out, full_bout = attn_gathered
    gain_two, shift_two, full_fc1, full_bfc1, full_fc2, full_bfc2 = mlp_gathered
    inputs_f = inputs.astype(jnp.float32)
    normed, inv_std = normalize(inputs_f)
    attn_in = (normed * gain_one.astype(jnp.float32) + shift_one.astype(jnp.float32)).astype(
        jnp.bfloat16
    )
    mlp_in = (normed * gain_two.astype(jnp.float32) + shift_two.astype(jnp.float32)).astype(
        jnp.bfloat16
    )
    joined = jnp.dot(attn_in, full_qkv, preferred_element_type=jnp.float32) + full_bqkv.astype(
        jnp.float32
    )
    joined = joined.reshape(row_count, 3, HEADS, HEAD)
    token_pos = cycle_place * row_count + jnp.arange(row_count, dtype=jnp.int32)
    cosine, sine_table = rotary_tables(token_pos.astype(jnp.float32), ROT)
    queries = rotate(joined[:, 0], cosine, sine_table, ROT).astype(jnp.bfloat16)
    keys_own = rotate(joined[:, 1], cosine, sine_table, ROT).astype(jnp.bfloat16)
    values_own = joined[:, 2].astype(jnp.bfloat16)
    row_top = jnp.full((HEADS, row_count), MASKED, jnp.float32)
    absorb_key_block = lax.all_gather(keys_own, "ctx", axis=0, tiled=True)
    absorb_value_block = lax.all_gather(values_own, "ctx", axis=0, tiled=True)
    absorb_key_pos = jnp.arange(absorb_key_block.shape[0], dtype=jnp.int32)
    absorb_visible = (token_pos[:, None] >= absorb_key_pos[None, :])[None]
    absorb_scores = (
        jnp.einsum("qhd,khd->hqk", queries, absorb_key_block, preferred_element_type=jnp.float32)
        * score_scale
    )
    absorb_scores = jnp.where(absorb_visible, absorb_scores, MASKED)
    new_top = jnp.maximum(row_top, jnp.max(absorb_scores, axis=-1))
    weights_exp = jnp.where(absorb_visible, jnp.exp(absorb_scores - new_top[:, :, None]), 0.0)
    row_total = jnp.sum(weights_exp, axis=-1)
    mixed = jnp.einsum(
        "hqk,khd->qhd",
        weights_exp.astype(jnp.bfloat16),
        absorb_value_block,
        preferred_element_type=jnp.float32,
    )
    row_top, row_total, mixed = (new_top, row_total, mixed)
    attended = (mixed / jnp.transpose(row_total)[:, :, None]).astype(jnp.bfloat16)
    log_total = row_top + jnp.log(row_total)
    attended_flat = attended.reshape(row_count, HEADS * HEAD)
    branch_attn = jnp.dot(
        attended_flat, full_out, preferred_element_type=jnp.float32
    ) + full_bout.astype(jnp.float32)
    preact = jnp.dot(mlp_in, full_fc1, preferred_element_type=jnp.float32) + full_bfc1.astype(
        jnp.float32
    )
    activated, slope = gelu_parts(preact)
    act_bf = activated.astype(jnp.bfloat16)
    branch_mlp = jnp.dot(act_bf, full_fc2, preferred_element_type=jnp.float32) + full_bfc2.astype(
        jnp.float32
    )
    output = (inputs_f + branch_attn + branch_mlp).astype(jnp.bfloat16)
    rows_all = (
        lax.all_gather(inputs, ("ctx", "fsdp"), axis=0, tiled=True),
        lax.all_gather(act_bf, ("ctx", "fsdp"), axis=0, tiled=True),
        lax.all_gather(attended_flat, ("ctx", "fsdp"), axis=0, tiled=True),
    )
    attn_gathered = (
        lax.all_gather(ln1_gain, ("ctx", "fsdp"), axis=0, tiled=True),
        lax.all_gather(ln1_bias, ("ctx", "fsdp"), axis=0, tiled=True),
        lax.all_gather(w_qkv, ("ctx", "fsdp"), axis=1, tiled=True),
        lax.all_gather(b_qkv, ("ctx", "fsdp"), axis=0, tiled=True),
        lax.all_gather(w_out, ("ctx", "fsdp"), axis=1, tiled=True),
        lax.all_gather(b_out, ("ctx", "fsdp"), axis=0, tiled=True),
    )
    mlp_gathered = (
        lax.all_gather(ln2_gain, ("ctx", "fsdp"), axis=0, tiled=True),
        lax.all_gather(ln2_bias, ("ctx", "fsdp"), axis=0, tiled=True),
        lax.all_gather(w_fc1, ("ctx", "fsdp"), axis=1, tiled=True),
        lax.all_gather(b_fc1, ("ctx", "fsdp"), axis=0, tiled=True),
        lax.all_gather(w_fc2, ("ctx", "fsdp"), axis=1, tiled=True),
        lax.all_gather(b_fc2, ("ctx", "fsdp"), axis=0, tiled=True),
    )
    gain_one, shift_one, full_qkv, full_bqkv, full_out, full_bout = attn_gathered
    gain_two, shift_two, full_fc1, full_bfc1, full_fc2, full_bfc2 = mlp_gathered
    upstream = upstream_bf.astype(jnp.float32)
    bias_out_grad = jnp.sum(upstream, axis=0)
    d_act = contract_cols(upstream_bf, full_fc2)
    d_preact = d_act * slope
    d_preact_bf = d_preact.astype(jnp.bfloat16)
    d_mlp_in = contract_cols(d_preact_bf, full_fc1)
    fc1_bias_grad = jnp.sum(d_preact, axis=0)
    ln2_gain_part = jnp.sum(d_mlp_in * normed, axis=0)
    ln2_bias_part = jnp.sum(d_mlp_in, axis=0)
    d_attended = (
        contract_cols(upstream_bf, full_out).astype(jnp.bfloat16).reshape(row_count, HEADS, HEAD)
    )
    row_dot = jnp.transpose(
        jnp.sum(d_attended.astype(jnp.float32) * attended.astype(jnp.float32), axis=-1)
    )
    d_queries = jnp.zeros((row_count, HEADS, HEAD), jnp.float32)
    travelling = (keys_own, values_own)
    key_grads = (
        jnp.zeros((row_count, HEADS, HEAD), jnp.float32),
        jnp.zeros((row_count, HEADS, HEAD), jnp.float32),
    )
    for turn_index in range(cycle_size):
        source = (cycle_place - turn_index) % cycle_size
        key_pos = source * row_count + jnp.arange(row_count, dtype=jnp.int32)
        key_block, value_block = travelling
        visible = (token_pos[:, None] >= key_pos[None, :])[None]
        scores = (
            jnp.einsum("qhd,khd->hqk", queries, key_block, preferred_element_type=jnp.float32)
            * score_scale
        )
        scores = jnp.where(visible, scores, MASKED)
        probability = jnp.where(visible, jnp.exp(scores - log_total[:, :, None]), 0.0)
        d_probability = jnp.einsum(
            "qhd,khd->hqk", d_attended, value_block, preferred_element_type=jnp.float32
        )
        d_scores = (probability * (d_probability - row_dot[:, :, None]) * score_scale).astype(
            jnp.bfloat16
        )
        d_queries = d_queries + jnp.einsum(
            "hqk,khd->qhd", d_scores, key_block, preferred_element_type=jnp.float32
        )
        key_grads = (
            key_grads[0]
            + jnp.einsum("hqk,qhd->khd", d_scores, queries, preferred_element_type=jnp.float32),
            key_grads[1]
            + jnp.einsum(
                "hqk,qhd->khd",
                probability.astype(jnp.bfloat16),
                d_attended,
                preferred_element_type=jnp.float32,
            ),
        )
        key_grads = from_behind((key_grads[0], key_grads[1]), "ctx", 1)
        if turn_index + 1 < cycle_size:
            travelling = shifted((travelling[0], travelling[1]), "ctx", 1)
    d_queries = rotate(d_queries, cosine, -sine_table, ROT)
    d_keys = rotate(key_grads[0], cosine, -sine_table, ROT)
    d_joined = jnp.stack([d_queries, d_keys, key_grads[1]], axis=1).reshape(
        row_count, 3 * HEADS * HEAD
    )
    d_joined_bf = d_joined.astype(jnp.bfloat16)
    d_attn_in = contract_cols(d_joined_bf, full_qkv)
    qkv_bias_grad = jnp.sum(d_joined, axis=0)
    ln1_gain_part = jnp.sum(d_attn_in * normed, axis=0)
    ln1_bias_part = jnp.sum(d_attn_in, axis=0)
    columns = (
        lax.all_to_all(upstream_bf, ("ctx", "fsdp"), split_axis=1, concat_axis=0, tiled=True),
        lax.all_to_all(d_preact_bf, ("ctx", "fsdp"), split_axis=1, concat_axis=0, tiled=True),
        lax.all_to_all(d_joined_bf, ("ctx", "fsdp"), split_axis=1, concat_axis=0, tiled=True),
    )
    small = (
        lax.psum_scatter(ln1_gain_part, ("ctx", "fsdp"), scatter_dimension=0, tiled=True),
        lax.psum_scatter(ln1_bias_part, ("ctx", "fsdp"), scatter_dimension=0, tiled=True),
        lax.psum_scatter(ln2_gain_part, ("ctx", "fsdp"), scatter_dimension=0, tiled=True),
        lax.psum_scatter(ln2_bias_part, ("ctx", "fsdp"), scatter_dimension=0, tiled=True),
        lax.psum_scatter(qkv_bias_grad, ("ctx", "fsdp"), scatter_dimension=0, tiled=True),
        lax.psum_scatter(bias_out_grad, ("ctx", "fsdp"), scatter_dimension=0, tiled=True),
        lax.psum_scatter(fc1_bias_grad, ("ctx", "fsdp"), scatter_dimension=0, tiled=True),
    )
    normed_all, unused_std = normalize(rows_all[0].astype(jnp.float32))
    attn_all = (normed_all * gain_one.astype(jnp.float32) + shift_one.astype(jnp.float32)).astype(
        jnp.bfloat16
    )
    mlp_all = (normed_all * gain_two.astype(jnp.float32) + shift_two.astype(jnp.float32)).astype(
        jnp.bfloat16
    )
    fc2_part = contract_rows(rows_all[1], columns[0])
    out_part = contract_rows(rows_all[2], columns[0])
    fc1_part = contract_rows(mlp_all, columns[1])
    qkv_part = contract_rows(attn_all, columns[2])
    owned = (
        small[0],
        small[1],
        small[2],
        small[3],
        qkv_part,
        small[4],
        out_part,
        small[5],
        fc1_part,
        small[6],
        fc2_part,
    )
    merged = d_attn_in * gain_one.astype(jnp.float32) + d_mlp_in * gain_two.astype(jnp.float32)
    input_grad = (upstream + norm_backward(merged, normed, inv_std)).astype(jnp.bfloat16)
    totals = lax.psum(
        (
            owned[0],
            owned[1],
            owned[2],
            owned[3],
            owned[4],
            owned[5],
            owned[6],
            owned[7],
            owned[8],
            owned[9],
            owned[10],
        ),
        "dp",
    )
    return (
        output[None],
        input_grad[None],
        totals[0],
        totals[1],
        totals[2],
        totals[3],
        totals[4],
        totals[5],
        totals[6],
        totals[7],
        totals[8],
        totals[9],
        totals[10],
        totals[7],
    )


def rotated(value, axis, steps):
    count = lax.axis_size(axis)
    return lax.ppermute(value, axis, [(i, (i + steps) % count) for i in range(count)])


def gather_rows(rows):
    ring = lax.axis_size("ctx")
    own = [rows] + [rotated(rows, "ctx", r) for r in range(1, ring)]
    other = [rotated(part, "fsdp", 1) for part in own]
    return jnp.concatenate(own + other, axis=0)


def scatter_rows(partial, ring):
    rows = partial.shape[0] // (2 * ring)
    total = None
    for r in reversed(range(ring)):
        mine = partial[r * rows : (r + 1) * rows]
        theirs = partial[(ring + r) * rows : (ring + r + 1) * rows]
        arrived = rotated(theirs.astype(jnp.bfloat16), "fsdp", 1)
        block = mine + arrived.astype(jnp.float32)
        if r:
            block = rotated(block.astype(jnp.bfloat16), "ctx", -r).astype(jnp.float32)
        total = block if total is None else total + block
    return total


def from_replicas(piece):
    x, core = lax.axis_index("x"), lax.axis_index("core")
    twin = rotated(piece, "core", 1)
    pair = jnp.where(core == 0, jnp.stack([piece, twin]), jnp.stack([twin, piece]))
    other = rotated(pair, "x", 1)
    return jnp.where(x == 0, jnp.stack([pair, other]), jnp.stack([other, pair]))


def replica_quarter(parts):
    x, core = lax.axis_index("x"), lax.axis_index("core")
    pick = lambda array, at, dim: lax.dynamic_index_in_dim(array, at, dim, keepdims=False)
    mine = pick(parts, core, 1) + rotated(pick(parts, 1 - core, 1), "core", 1)
    sent = rotated(pick(mine, 1 - x, 0).astype(jnp.bfloat16), "x", 1)
    return pick(mine, x, 0) + sent.astype(jnp.float32)


def tensor_body(
    hidden,
    cotangent,
    ln1_gain,
    ln1_bias,
    ln2_gain,
    ln2_bias,
    w_qkv,
    b_qkv,
    w_out,
    b_out,
    w_fc1,
    b_fc1,
    w_fc2,
    b_fc2,
):
    f32, bf16 = jnp.float32, jnp.bfloat16
    group = ("ctx", "fsdp")
    ring = lax.axis_size("ctx")
    members = ring * lax.axis_size("fsdp")
    place = lax.axis_index(group)
    replica = lax.axis_index(("x", "core"))
    inputs, upstream_own = hidden[0], cotangent[0]
    row_count, width = inputs.shape
    length = ring * row_count
    cols = width // members
    units = w_fc1.shape[1]
    slots = w_qkv.shape[1] // HEAD
    score_scale = HEAD ** (-0.5)

    def quarter(array, dim):
        size = array.shape[dim] // 4
        return lax.dynamic_slice_in_dim(array, replica * size, size, dim)

    rows = gather_rows(inputs)
    small = jnp.concatenate([ln1_gain, ln1_bias, ln2_gain, ln2_bias, b_out, b_fc2, b_qkv])
    small = lax.all_gather(small, group, axis=0, tiled=False).astype(f32)
    gain_one, shift_one, gain_two, shift_two, full_bout, full_bfc2 = (
        small[:, i * cols : (i + 1) * cols].reshape(width) for i in range(6)
    )
    full_bqkv = small[:, 6 * cols :].reshape(3 * HEADS, HEAD)

    qkv_quarter = quarter(w_qkv, 0)
    qkv_moved = [
        lax.ppermute(
            qkv_quarter[:, s * HEAD : (s + 1) * HEAD],
            group,
            [(i, (slots * i + s) % members) for i in range(members)],
        )
        for s in range(slots)
    ]
    head_qkv = from_replicas(jnp.concatenate(qkv_moved, axis=1)).reshape(width, slots * HEAD)

    moved = jnp.concatenate(
        [
            quarter(w_fc2.reshape(members, units, cols), 1),
            quarter(w_out.reshape(members, HEAD, cols), 1),
        ],
        axis=1,
    )
    moved = lax.all_to_all(moved, group, split_axis=0, concat_axis=0, tiled=True)
    moved = from_replicas(moved).reshape(4, members, (units + HEAD) // 4, cols)
    rows_fc2 = jnp.transpose(moved[:, :, : units // 4], (0, 2, 1, 3)).reshape(units, width)
    rows_out = jnp.transpose(moved[:, :, units // 4 :], (0, 2, 1, 3)).reshape(HEAD, width)

    upstream = gather_rows(upstream_own)

    kind_of = [[0] * slots for _ in range(members)]
    slot_of = [[0] * slots for _ in range(members)]
    for source in range(members):
        for s in range(slots):
            block = slots * source + s
            kind_of[block % members][s] = block // HEADS
            slot_of[block % members][block // HEADS] = s
    kinds = jnp.asarray(kind_of, jnp.int32)[place]
    where_is = jnp.asarray(slot_of, jnp.int32)[place]

    inputs_f = rows.astype(f32)
    normed, _ = normalize(inputs_f)
    attn_in = (normed * gain_one + shift_one).astype(bf16)
    mlp_in = (normed * gain_two + shift_two).astype(bf16)

    joined = jnp.dot(attn_in, head_qkv, preferred_element_type=f32)
    bias_rows = kinds * HEADS + place
    joined = joined.reshape(2, length, slots, HEAD) + full_bqkv[bias_rows]
    token_pos = (
        ((lax.axis_index("ctx") - jnp.arange(ring)) % ring)[:, None] * row_count
        + jnp.arange(row_count)[None]
    ).reshape(length)
    cosine, sine_table = rotary_tables(token_pos.astype(f32), ROT)
    cosine, sine_table = cosine[None, :, 0], sine_table[None, :, 0]
    pick = lambda kind: lax.dynamic_index_in_dim(joined, where_is[kind], 2, keepdims=False)
    queries = rotate(pick(0), cosine, sine_table, ROT).astype(bf16)
    keys = rotate(pick(1), cosine, sine_table, ROT).astype(bf16)
    values = pick(2).astype(bf16)
    visible = (token_pos[:, None] >= token_pos[None, :])[None]
    scores = jnp.einsum("sqd,skd->sqk", queries, keys, preferred_element_type=f32) * score_scale
    scores = jnp.where(visible, scores, MASKED)
    row_top = jnp.max(scores, axis=-1, keepdims=True)
    weights_exp = jnp.where(visible, jnp.exp(scores - row_top), 0.0)
    row_total = jnp.sum(weights_exp, axis=-1, keepdims=True)
    mixed = jnp.einsum("sqk,skd->sqd", weights_exp.astype(bf16), values, preferred_element_type=f32)
    attended = (mixed / row_total).astype(bf16)
    log_total = row_top + jnp.log(row_total)
    attended_flat = attended.reshape(2 * length, HEAD)

    preact = jnp.dot(mlp_in, w_fc1, preferred_element_type=f32) + b_fc1.astype(f32)
    activated, slope = gelu_parts(preact)
    act_bf = activated.astype(bf16)
    branch = jnp.dot(attended_flat, rows_out, preferred_element_type=f32) + jnp.dot(
        act_bf, rows_fc2, preferred_element_type=f32
    )
    branch = scatter_rows(branch, ring)
    own_f = inputs.astype(f32)
    output = (own_f + (branch + full_bout + full_bfc2)).astype(bf16)

    d_act = contract_cols(upstream, rows_fc2)
    d_preact = d_act * slope
    d_preact_bf = d_preact.astype(bf16)
    fc1_bias_part = jnp.sum(d_preact, axis=0)
    d_mlp_in = contract_cols(d_preact_bf, w_fc1)
    d_attended = contract_cols(upstream, rows_out).astype(bf16).reshape(2, length, HEAD)
    row_dot = jnp.sum(d_attended.astype(f32) * attended.astype(f32), axis=-1, keepdims=True)
    probability = jnp.where(visible, jnp.exp(scores - log_total), 0.0)
    d_probability = jnp.einsum("sqd,skd->sqk", d_attended, values, preferred_element_type=f32)
    d_scores = (probability * (d_probability - row_dot) * score_scale).astype(bf16)
    d_queries = jnp.einsum("sqk,skd->sqd", d_scores, keys, preferred_element_type=f32)
    d_keys = jnp.einsum("sqk,sqd->skd", d_scores, queries, preferred_element_type=f32)
    d_values = jnp.einsum(
        "sqk,sqd->skd", probability.astype(bf16), d_attended, preferred_element_type=f32
    )
    d_queries = rotate(d_queries, cosine, -sine_table, ROT).reshape(2 * length, HEAD)
    d_keys = rotate(d_keys, cosine, -sine_table, ROT).reshape(2 * length, HEAD)
    d_values = d_values.reshape(2 * length, HEAD)
    by_kind = (d_queries, d_keys, d_values)
    bias_kind = jnp.stack([jnp.sum(grad, axis=0) for grad in by_kind])
    by_kind = jnp.stack([grad.astype(bf16) for grad in by_kind])
    d_joined_bf = jnp.concatenate(
        [lax.dynamic_index_in_dim(by_kind, kinds[s], 0, keepdims=False) for s in range(slots)], axis=1
    )
    d_attn_in = contract_cols(d_joined_bf, head_qkv)

    merged = scatter_rows(d_attn_in * gain_one + d_mlp_in * gain_two, ring)
    own_normed, own_std = normalize(own_f)
    input_grad = (
        upstream_own.astype(f32) + norm_backward(merged, own_normed, own_std)
    ).astype(bf16)

    bqkv_all = jnp.zeros((3, HEADS, HEAD), f32)
    bqkv_all = lax.dynamic_update_slice(bqkv_all, bias_kind[:, None], (0, place, 0))
    upstream_sum = jnp.sum(upstream_own.astype(f32), axis=0)
    vectors = [
        jnp.sum(d_attn_in * normed, axis=0),
        jnp.sum(d_attn_in, axis=0),
        jnp.sum(d_mlp_in * normed, axis=0),
        jnp.sum(d_mlp_in, axis=0),
        upstream_sum,
        bqkv_all.reshape(3 * width),
    ]
    vectors = jnp.concatenate([v.reshape(members, -1) for v in vectors], axis=1)
    fc1_all = lax.dynamic_update_slice(
        jnp.zeros((members, units), f32), fc1_bias_part[None], (place, 0)
    )
    vectors = lax.psum(
        jnp.concatenate([vectors, fc1_all], axis=1), ("x", "core", "ctx", "fsdp")
    )
    vectors = lax.dynamic_index_in_dim(vectors, place, 0, keepdims=False)
    g1, s1, g2, s2, bout_grad = (vectors[i * cols : (i + 1) * cols] for i in range(5))
    bqkv_grad = vectors[5 * cols : 5 * cols + slots * HEAD]
    bfc1_grad = vectors[5 * cols + slots * HEAD :]

    fc2_part = contract_rows(act_bf, upstream).reshape(2, 2, units // 4, width)
    out_part = contract_rows(attended_flat, upstream).reshape(2, 2, HEAD // 4, width)
    rows_part = replica_quarter(jnp.concatenate([fc2_part, out_part], axis=2))
    rows_part = rows_part.astype(bf16).reshape(-1, members, cols)
    back = lax.all_to_all(
        jnp.transpose(rows_part, (1, 0, 2)), group, split_axis=0, concat_axis=0, tiled=True
    )
    back = from_replicas(back).reshape(4, members, (units + HEAD) // 4, cols)
    fc2_grad = jnp.transpose(back[:, :, : units // 4], (1, 0, 2, 3)).reshape(-1, cols).astype(f32)
    out_grad = jnp.transpose(back[:, :, units // 4 :], (1, 0, 2, 3)).reshape(-1, cols).astype(f32)

    fc1_part = contract_rows(mlp_in, d_preact_bf).reshape(2, width // 2, units)
    core = lax.axis_index("core")
    half = lax.dynamic_index_in_dim(fc1_part, core, 0, keepdims=False) + rotated(
        lax.dynamic_index_in_dim(fc1_part, 1 - core, 0, keepdims=False), "core", 1
    )
    half = half.astype(bf16)
    half = half.astype(f32) + rotated(half, "x", 1).astype(f32)
    twin = rotated(half, "core", 1)
    fc1_grad = jnp.where(core == 0, jnp.stack([half, twin]), jnp.stack([twin, half]))
    fc1_grad = fc1_grad.reshape(width, units)

    qkv_part = contract_rows(attn_in, d_joined_bf).reshape(2, 2, width // 4, slots * HEAD)
    qkv_part = replica_quarter(qkv_part).astype(bf16)
    qkv_back = [
        lax.ppermute(
            qkv_part[:, s * HEAD : (s + 1) * HEAD],
            group,
            [((slots * i + s) % members, i) for i in range(members)],
        )
        for s in range(slots)
    ]
    qkv_grad = from_replicas(jnp.concatenate(qkv_back, axis=1)).reshape(width, -1).astype(f32)

    return (
        output[None],
        input_grad[None],
        g1,
        s1,
        g2,
        s2,
        qkv_grad,
        bqkv_grad,
        out_grad,
        bout_grad,
        fc1_grad,
        bfc1_grad,
        fc2_grad,
        bout_grad,
    )


def solution(mesh):
    sizes = dict(mesh.shape)
    x_size = sizes["dp"] // 2
    fits = sizes["ctx"] * sizes["fsdp"] == HEADS and sizes["fsdp"] == 2 and sizes["dp"] == 4
    if fits:
        mesh = Mesh(
            mesh.devices.reshape(x_size, 2, sizes["ctx"], sizes["fsdp"]),
            ("x", "core", "ctx", "fsdp"),
        )
        dp = ("x", "core")
    else:
        dp = ("dp",)
    rows = P((*dp, "fsdp"), "ctx", None)
    vector, matrix = P(("ctx", "fsdp")), P(None, ("ctx", "fsdp"))
    params = (vector,) * 4 + (matrix, vector) * 4
    return jax.shard_map(
        tensor_body if fits else body,
        mesh=mesh,
        in_specs=(rows, rows, *params),
        out_specs=(rows, rows, *params),
        check_vma=False,
    )
```

```python
import math

import jax
import jax.numpy as jnp
from jax import lax
from jax.experimental import pallas as pl
from jax.experimental.pallas import tpu as pltpu
from jax.sharding import Mesh
from jax.sharding import PartitionSpec as P

HEADS = 8
HEAD = 256
ROT = 64


EPSILON = 1e-05
SQRT_HALF = 0.7071067811865476
INV_ROOT_TWO_PI = 0.3989422804014327
MASKED = -1e30

DP, CTX, FSDP, X, CORE = "dp", "ctx", "fsdp", "x", "core"
GROUP, REPLICAS = (CTX, FSDP), (X, CORE)
QK, KV, QT = "qhd,khd->hqk", "hqk,khd->qhd", "hqk,qhd->khd"


def from_behind(value, axis, steps):
    count = lax.axis_size(axis)
    pairs = [(source, (source + steps) % count) for source in range(count)]
    return lax.ppermute(value, axis, pairs)


def shifted(block, axis, distance):
    devices = range(lax.axis_size(axis))
    route = [(i - distance, i) for i in devices if i - distance in devices]
    return lax.ppermute(block, axis, route)


def normalize(inputs):
    centre = jnp.mean(inputs, axis=-1, keepdims=True)
    centred = inputs - centre
    variance = jnp.mean(centred * centred, axis=-1, keepdims=True)
    inv_std = lax.rsqrt(variance + EPSILON)
    return (centred * inv_std, inv_std)


def norm_backward(upstream, normed, inv_std):
    first_mean = jnp.mean(upstream, axis=-1, keepdims=True)
    second_mean = jnp.mean(upstream * normed, axis=-1, keepdims=True)
    return inv_std * (upstream - first_mean - normed * second_mean)


def gelu_parts(preact):
    normal_cdf = 0.5 * (1.0 + lax.erf(preact * SQRT_HALF))
    normal_pdf = jnp.exp(-0.5 * preact * preact) * INV_ROOT_TWO_PI
    return (preact * normal_cdf, normal_cdf + preact * normal_pdf)


def rotary_tables(positions, rot_dims):
    half_dims = rot_dims // 2
    frequency = jnp.exp(
        jnp.arange(half_dims).astype(jnp.float32) * (-2.0 * math.log(10000.0) / rot_dims)
    )
    angles = positions[:, None] * frequency[None, :]
    return (jnp.cos(angles)[:, None, :], jnp.sin(angles)[:, None, :])


def rotate(tensor, cosine, sine_table, rot_dims):
    half_dims = rot_dims // 2
    leading = tensor[..., :half_dims]
    trailing = tensor[..., half_dims:rot_dims]
    return jnp.concatenate(
        [
            leading * cosine - trailing * sine_table,
            trailing * cosine + leading * sine_table,
            tensor[..., rot_dims:],
        ],
        axis=-1,
    )


def contract_rows(left, right):
    return lax.dot_general(
        left, right, (((0,), (0,)), ((), ())), preferred_element_type=jnp.float32
    )


def contract_cols(left, right):
    return lax.dot_general(
        left, right, (((1,), (1,)), ((), ())), preferred_element_type=jnp.float32
    )


def plain_layer(
    hidden,
    cotangent,
    ln1_gain,
    ln1_bias,
    ln2_gain,
    ln2_bias,
    w_qkv,
    b_qkv,
    w_out,
    b_out,
    w_fc1,
    b_fc1,
    w_fc2,
    b_fc2,
):
    inputs = hidden[0]
    upstream_bf = cotangent[0]
    row_count = inputs.shape[0]
    score_scale = HEAD ** (-0.5)
    cycle_size = lax.axis_size(CTX)
    cycle_place = lax.axis_index(CTX)
    attn_gathered = (
        lax.all_gather(ln1_gain, GROUP, axis=0, tiled=True),
        lax.all_gather(ln1_bias, GROUP, axis=0, tiled=True),
        lax.all_gather(w_qkv, GROUP, axis=1, tiled=True),
        lax.all_gather(b_qkv, GROUP, axis=0, tiled=True),
        lax.all_gather(w_out, GROUP, axis=1, tiled=True),
        lax.all_gather(b_out, GROUP, axis=0, tiled=True),
    )
    mlp_gathered = (
        lax.all_gather(ln2_gain, GROUP, axis=0, tiled=True),
        lax.all_gather(ln2_bias, GROUP, axis=0, tiled=True),
        lax.all_gather(w_fc1, GROUP, axis=1, tiled=True),
        lax.all_gather(b_fc1, GROUP, axis=0, tiled=True),
        lax.all_gather(w_fc2, GROUP, axis=1, tiled=True),
        lax.all_gather(b_fc2, GROUP, axis=0, tiled=True),
    )
    gain_one, shift_one, full_qkv, full_bqkv, full_out, full_bout = attn_gathered
    gain_two, shift_two, full_fc1, full_bfc1, full_fc2, full_bfc2 = mlp_gathered
    inputs_f = inputs.astype(jnp.float32)
    normed, inv_std = normalize(inputs_f)
    attn_in = (normed * gain_one.astype(jnp.float32) + shift_one.astype(jnp.float32)).astype(
        jnp.bfloat16
    )
    mlp_in = (normed * gain_two.astype(jnp.float32) + shift_two.astype(jnp.float32)).astype(
        jnp.bfloat16
    )
    joined = jnp.dot(attn_in, full_qkv, preferred_element_type=jnp.float32) + full_bqkv.astype(
        jnp.float32
    )
    joined = joined.reshape(row_count, 3, HEADS, HEAD)
    token_pos = cycle_place * row_count + jnp.arange(row_count, dtype=jnp.int32)
    cosine, sine_table = rotary_tables(token_pos.astype(jnp.float32), ROT)
    queries = rotate(joined[:, 0], cosine, sine_table, ROT).astype(jnp.bfloat16)
    keys_own = rotate(joined[:, 1], cosine, sine_table, ROT).astype(jnp.bfloat16)
    values_own = joined[:, 2].astype(jnp.bfloat16)
    row_top = jnp.full((HEADS, row_count), MASKED, jnp.float32)
    absorb_key_block = lax.all_gather(keys_own, CTX, axis=0, tiled=True)
    absorb_value_block = lax.all_gather(values_own, CTX, axis=0, tiled=True)
    absorb_key_pos = jnp.arange(absorb_key_block.shape[0], dtype=jnp.int32)
    absorb_visible = (token_pos[:, None] >= absorb_key_pos[None, :])[None]
    absorb_scores = (
        jnp.einsum(QK, queries, absorb_key_block, preferred_element_type=jnp.float32)
        * score_scale
    )
    absorb_scores = jnp.where(absorb_visible, absorb_scores, MASKED)
    new_top = jnp.maximum(row_top, jnp.max(absorb_scores, axis=-1))
    weights_exp = jnp.where(absorb_visible, jnp.exp(absorb_scores - new_top[:, :, None]), 0.0)
    row_total = jnp.sum(weights_exp, axis=-1)
    mixed = jnp.einsum(
        KV,
        weights_exp.astype(jnp.bfloat16),
        absorb_value_block,
        preferred_element_type=jnp.float32,
    )
    row_top, row_total, mixed = (new_top, row_total, mixed)
    attended = (mixed / jnp.transpose(row_total)[:, :, None]).astype(jnp.bfloat16)
    log_total = row_top + jnp.log(row_total)
    attended_flat = attended.reshape(row_count, HEADS * HEAD)
    branch_attn = jnp.dot(
        attended_flat, full_out, preferred_element_type=jnp.float32
    ) + full_bout.astype(jnp.float32)
    preact = jnp.dot(mlp_in, full_fc1, preferred_element_type=jnp.float32) + full_bfc1.astype(
        jnp.float32
    )
    activated, slope = gelu_parts(preact)
    act_bf = activated.astype(jnp.bfloat16)
    branch_mlp = jnp.dot(act_bf, full_fc2, preferred_element_type=jnp.float32) + full_bfc2.astype(
        jnp.float32
    )
    output = (inputs_f + branch_attn + branch_mlp).astype(jnp.bfloat16)
    rows_all = (
        lax.all_gather(inputs, GROUP, axis=0, tiled=True),
        lax.all_gather(act_bf, GROUP, axis=0, tiled=True),
        lax.all_gather(attended_flat, GROUP, axis=0, tiled=True),
    )
    attn_gathered = (
        lax.all_gather(ln1_gain, GROUP, axis=0, tiled=True),
        lax.all_gather(ln1_bias, GROUP, axis=0, tiled=True),
        lax.all_gather(w_qkv, GROUP, axis=1, tiled=True),
        lax.all_gather(b_qkv, GROUP, axis=0, tiled=True),
        lax.all_gather(w_out, GROUP, axis=1, tiled=True),
        lax.all_gather(b_out, GROUP, axis=0, tiled=True),
    )
    mlp_gathered = (
        lax.all_gather(ln2_gain, GROUP, axis=0, tiled=True),
        lax.all_gather(ln2_bias, GROUP, axis=0, tiled=True),
        lax.all_gather(w_fc1, GROUP, axis=1, tiled=True),
        lax.all_gather(b_fc1, GROUP, axis=0, tiled=True),
        lax.all_gather(w_fc2, GROUP, axis=1, tiled=True),
        lax.all_gather(b_fc2, GROUP, axis=0, tiled=True),
    )
    gain_one, shift_one, full_qkv, full_bqkv, full_out, full_bout = attn_gathered
    gain_two, shift_two, full_fc1, full_bfc1, full_fc2, full_bfc2 = mlp_gathered
    upstream = upstream_bf.astype(jnp.float32)
    bias_out_grad = jnp.sum(upstream, axis=0)
    d_act = contract_cols(upstream_bf, full_fc2)
    d_preact = d_act * slope
    d_preact_bf = d_preact.astype(jnp.bfloat16)
    d_mlp_in = contract_cols(d_preact_bf, full_fc1)
    fc1_bias_grad = jnp.sum(d_preact, axis=0)
    ln2_gain_part = jnp.sum(d_mlp_in * normed, axis=0)
    ln2_bias_part = jnp.sum(d_mlp_in, axis=0)
    d_attended = (
        contract_cols(upstream_bf, full_out).astype(jnp.bfloat16).reshape(row_count, HEADS, HEAD)
    )
    row_dot = jnp.transpose(
        jnp.sum(d_attended.astype(jnp.float32) * attended.astype(jnp.float32), axis=-1)
    )
    d_queries = jnp.zeros((row_count, HEADS, HEAD), jnp.float32)
    travelling = (keys_own, values_own)
    key_grads = (
        jnp.zeros((row_count, HEADS, HEAD), jnp.float32),
        jnp.zeros((row_count, HEADS, HEAD), jnp.float32),
    )
    for turn_index in range(cycle_size):
        source = (cycle_place - turn_index) % cycle_size
        key_pos = source * row_count + jnp.arange(row_count, dtype=jnp.int32)
        key_block, value_block = travelling
        visible = (token_pos[:, None] >= key_pos[None, :])[None]
        scores = (
            jnp.einsum(QK, queries, key_block, preferred_element_type=jnp.float32)
            * score_scale
        )
        scores = jnp.where(visible, scores, MASKED)
        probability = jnp.where(visible, jnp.exp(scores - log_total[:, :, None]), 0.0)
        d_probability = jnp.einsum(
            QK, d_attended, value_block, preferred_element_type=jnp.float32
        )
        d_scores = (probability * (d_probability - row_dot[:, :, None]) * score_scale).astype(
            jnp.bfloat16
        )
        d_queries = d_queries + jnp.einsum(
            KV, d_scores, key_block, preferred_element_type=jnp.float32
        )
        key_grads = (
            key_grads[0]
            + jnp.einsum(QT, d_scores, queries, preferred_element_type=jnp.float32),
            key_grads[1]
            + jnp.einsum(
                QT,
                probability.astype(jnp.bfloat16),
                d_attended,
                preferred_element_type=jnp.float32,
            ),
        )
        key_grads = from_behind((key_grads[0], key_grads[1]), CTX, 1)
        if turn_index + 1 < cycle_size:
            travelling = shifted((travelling[0], travelling[1]), CTX, 1)
    d_queries = rotate(d_queries, cosine, -sine_table, ROT)
    d_keys = rotate(key_grads[0], cosine, -sine_table, ROT)
    d_joined = jnp.stack([d_queries, d_keys, key_grads[1]], axis=1).reshape(
        row_count, 3 * HEADS * HEAD
    )
    d_joined_bf = d_joined.astype(jnp.bfloat16)
    d_attn_in = contract_cols(d_joined_bf, full_qkv)
    qkv_bias_grad = jnp.sum(d_joined, axis=0)
    ln1_gain_part = jnp.sum(d_attn_in * normed, axis=0)
    ln1_bias_part = jnp.sum(d_attn_in, axis=0)
    columns = (
        lax.all_to_all(upstream_bf, GROUP, split_axis=1, concat_axis=0, tiled=True),
        lax.all_to_all(d_preact_bf, GROUP, split_axis=1, concat_axis=0, tiled=True),
        lax.all_to_all(d_joined_bf, GROUP, split_axis=1, concat_axis=0, tiled=True),
    )
    small = (
        lax.psum_scatter(ln1_gain_part, GROUP, scatter_dimension=0, tiled=True),
        lax.psum_scatter(ln1_bias_part, GROUP, scatter_dimension=0, tiled=True),
        lax.psum_scatter(ln2_gain_part, GROUP, scatter_dimension=0, tiled=True),
        lax.psum_scatter(ln2_bias_part, GROUP, scatter_dimension=0, tiled=True),
        lax.psum_scatter(qkv_bias_grad, GROUP, scatter_dimension=0, tiled=True),
        lax.psum_scatter(bias_out_grad, GROUP, scatter_dimension=0, tiled=True),
        lax.psum_scatter(fc1_bias_grad, GROUP, scatter_dimension=0, tiled=True),
    )
    normed_all, _ = normalize(rows_all[0].astype(jnp.float32))
    attn_all = (normed_all * gain_one.astype(jnp.float32) + shift_one.astype(jnp.float32)).astype(
        jnp.bfloat16
    )
    mlp_all = (normed_all * gain_two.astype(jnp.float32) + shift_two.astype(jnp.float32)).astype(
        jnp.bfloat16
    )
    fc2_part = contract_rows(rows_all[1], columns[0])
    out_part = contract_rows(rows_all[2], columns[0])
    fc1_part = contract_rows(mlp_all, columns[1])
    qkv_part = contract_rows(attn_all, columns[2])
    owned = (
        small[0],
        small[1],
        small[2],
        small[3],
        qkv_part,
        small[4],
        out_part,
        small[5],
        fc1_part,
        small[6],
        fc2_part,
    )
    merged = d_attn_in * gain_one.astype(jnp.float32) + d_mlp_in * gain_two.astype(jnp.float32)
    input_grad = (upstream + norm_backward(merged, normed, inv_std)).astype(jnp.bfloat16)
    totals = lax.psum(
        (
            owned[0],
            owned[1],
            owned[2],
            owned[3],
            owned[4],
            owned[5],
            owned[6],
            owned[7],
            owned[8],
            owned[9],
            owned[10],
        ),
        DP,
    )
    return (
        output[None],
        input_grad[None],
        totals[0],
        totals[1],
        totals[2],
        totals[3],
        totals[4],
        totals[5],
        totals[6],
        totals[7],
        totals[8],
        totals[9],
        totals[10],
        totals[7],
    )


def rotated(value, axis, steps):
    count = lax.axis_size(axis)
    return lax.ppermute(value, axis, [(i, (i + steps) % count) for i in range(count)])


def gather_line(block):
    place = lax.axis_index(CTX)
    low = rotated(block, CTX, 1)
    high = rotated(block, CTX, 3)
    up = lax.ppermute(low, CTX, [(1, 2), (2, 3)])
    down = lax.ppermute(high, CTX, [(2, 1), (1, 0)])
    middle = jnp.where(place >= 2, up, down)
    return [block, low, middle, high]


def gather_side(blocks):
    gathered = []
    for block in blocks:
        gathered.append(rotated(block, FSDP, 1))
    return gathered


NT = (((1,), (1,)), ((), ()))
TN = (((0,), (0,)), ((), ()))
NN = (((1,), (0,)), ((), ()))
ROPE_LANES = 128
VMEM_LIMIT = 16 << 20


def mm(left, right, dims=NN):
    return lax.dot_general(left, right, dims, preferred_element_type=jnp.float32)


def whole(shape):
    return pl.BlockSpec(shape, lambda *_: (0,) * len(shape), pipeline_mode=pl.Buffered(1))


def call(kernel, grid, in_specs, out_specs, outs, scratch=(), scalars=(), args=()):
    return pl.pallas_call(
        kernel,
        grid_spec=pltpu.PrefetchScalarGridSpec(
            num_scalar_prefetch=len(scalars),
            grid=grid,
            in_specs=in_specs,
            out_specs=out_specs,
            scratch_shapes=list(scratch),
        ),
        out_shape=[jax.ShapeDtypeStruct(shape, dtype) for shape, dtype in outs],
        compiler_params=pltpu.CompilerParams(vmem_limit_bytes=VMEM_LIMIT),
    )(*scalars, *args)


def pack_columns(pieces):
    rows = pieces[0].shape[0]
    total = sum(p.shape[1] for p in pieces)

    def kernel(*refs):
        begin = 0
        for ref in refs[:-1]:
            end = begin + ref.shape[1]
            refs[-1][:, begin:end] = ref[...]
            begin = end

    return call(
        kernel,
        (1,),
        [whole(p.shape) for p in pieces],
        [whole((rows, total))],
        [((rows, total), pieces[0].dtype)],
        args=pieces,
    )[0]


def norm_fc1(pieces, params, w_fc1, b_fc1):
    f32, bf16 = jnp.float32, jnp.bfloat16
    count, (piece, width) = len(pieces), pieces[0].shape
    rows, units = count * piece, w_fc1.shape[1]
    chunk, step, tall = 256, 64, 256

    def kernel(*refs):
        piece_refs, (par, w, b, attn, mlp, centre, scale, act, slope) = refs[:count], refs[count:]

        @pl.when(pl.program_id(0) == 0)
        def _():
            for i in range(count):

                def norm(k, _, i=i):
                    x = piece_refs[i][pl.ds(pl.multiple_of(k * step, step), step), :].astype(f32)
                    mean = jnp.mean(x, axis=-1, keepdims=True)
                    x = x - mean
                    inv = lax.rsqrt(jnp.mean(x * x, axis=-1, keepdims=True) + EPSILON)
                    x = x * inv
                    here = pl.ds(pl.multiple_of(i * piece + k * step, step), step)
                    attn[here, :] = (x * par[0:1] + par[1:2]).astype(bf16)
                    mlp[here, :] = (x * par[2:3] + par[3:4]).astype(bf16)
                    centre[here, :] = mean
                    scale[here, :] = inv
                    return 0

                lax.fori_loop(0, piece // step, norm, 0)

        for r in range(rows // tall):
            here = slice(r * tall, (r + 1) * tall)
            activated, gradient = gelu_parts(mm(mlp[here, :], w[...]) + b[...])
            act[here, :] = activated.astype(bf16)
            slope[here, :] = gradient

    column = pl.BlockSpec((rows, chunk), lambda j: (0, j))
    return call(
        kernel,
        (units // chunk,),
        [whole((piece, width))] * count
        + [
            whole(params.shape),
            pl.BlockSpec((width, chunk), lambda j: (0, j)),
            pl.BlockSpec((1, chunk), lambda j: (0, j)),
        ],
        [whole((rows, width))] * 2 + [whole((rows, 1))] * 2 + [column] * 2,
        [((rows, width), bf16)] * 2
        + [((rows, 1), f32)] * 2
        + [((rows, units), bf16), ((rows, units), f32)],
        args=(*pieces, params, w_fc1, b_fc1),
    )


def turn(tensor, cosine, sine):
    first = tensor[:, :ROPE_LANES]
    lane = lax.broadcasted_iota(jnp.int32, first.shape, 1)
    swapped = jnp.where(
        lane < ROT // 2,
        pltpu.roll(first, ROPE_LANES - ROT // 2, 1),
        pltpu.roll(first, ROT // 2, 1),
    )
    return jnp.concatenate([first * cosine + swapped * sine, tensor[:, ROPE_LANES:]], axis=1)


def head_attention(attn_in, weights, bias, tables, positions, meta):
    f32, bf16 = jnp.float32, jnp.bfloat16
    length, width = attn_in.shape
    chunk, slots = length // 4, 3
    joins = len(weights) > 1

    def kernel(meta, x, *refs):
        pieces, (b, cosine, sine, down, along) = refs[: len(weights)], refs[len(weights) :][:5]
        qkv, att, log_total = refs[-3:]
        w = refs[-4] if joins else pieces[0]
        if joins:
            deep = pieces[0].shape[0]
            for d, p in enumerate(pieces):
                here = pl.ds(pl.multiple_of((meta[0] ^ d) * deep, deep), deep)
                for s in range(slots):
                    w[meta[1 + s], here, :] = p[:, s * HEAD : (s + 1) * HEAD]
        for kind in range(3):
            t = mm(x[...], w[kind]) + b[kind]
            if kind < 2:
                t = turn(t, cosine[...], sine[...])
            qkv[kind] = t.astype(bf16)
        for c in range(4):
            here = slice(c * chunk, (c + 1) * chunk)
            seen = down[here, :] >= along[...]
            scores = jnp.where(seen, mm(qkv[0, here, :], qkv[1], NT) * HEAD**-0.5, MASKED)
            top = jnp.max(scores, axis=-1, keepdims=True)
            powers = jnp.where(seen, jnp.exp(scores - top), 0.0)
            total = jnp.sum(powers, axis=-1, keepdims=True)
            att[here, :] = (mm(powers.astype(bf16), qkv[2]) / total).astype(bf16)
            log_total[here, :] = top + jnp.log(total)

    args = (attn_in, *weights, bias, *tables, *positions)
    outs = [((3, length, HEAD), bf16), ((length, HEAD), bf16), ((length, 1), f32)]
    if joins:
        outs = [((3, width, HEAD), bf16)] + outs
    return call(
        kernel,
        (1,),
        [whole(v.shape) for v in args],
        [whole(shape) for shape, _ in outs],
        outs,
        scalars=(meta,),
        args=args,
    )


def project_other(pieces, act, att, meta):
    bf16 = jnp.bfloat16
    members, _, cols = pieces[0].shape
    length, units = act.shape
    width = members * cols
    tall, low = units // 4, HEAD // 4

    def kernel(meta, p0, p1, p2, p3, act, att, w, out):
        for d, p in enumerate((p0, p1, p2, p3)):
            q = meta[0] ^ d
            upper = pl.ds(pl.multiple_of(q * tall, tall), tall)
            lower = pl.ds(pl.multiple_of(units + q * low, low), low)
            for m in range(members):
                w[upper, m * cols : (m + 1) * cols] = p[m, :tall, :]
                w[lower, m * cols : (m + 1) * cols] = p[m, tall:, :]
        for m in range(members):
            here = slice(m * cols, (m + 1) * cols)
            part = mm(act[...], w[:units, here]) + mm(att[...], w[units:, here])
            out[:, here] = part.astype(bf16)

    args = (*pieces, act, att)
    return call(
        kernel,
        (1,),
        [whole(v.shape) for v in args],
        [whole((units + HEAD, width)), whole((length, width))],
        [((units + HEAD, width), bf16), ((length, width), bf16)],
        scalars=(meta,),
        args=args,
    )


def project_own(w, act, att):
    length, units = act.shape
    width, chunk = w.shape[1], 512

    def kernel(w, act, att, out, both):
        @pl.when(pl.program_id(0) == 0)
        def _():
            both[:, :units] = act[...]
            both[:, units:] = att[...]

        out[...] = mm(both[...], w[...]).astype(out.dtype)

    return call(
        kernel,
        (width // chunk,),
        [pl.BlockSpec((units + HEAD, chunk), lambda j: (0, j)), whole(act.shape), whole(att.shape)],
        [pl.BlockSpec((length, chunk), lambda j: (0, j))],
        [((length, width), jnp.bfloat16)],
        [pltpu.VMEM((length, units + HEAD), jnp.bfloat16)],
        args=(w, act, att),
    )[0]


def backward(cot, w, slope, att, qkv, log_total, tables, positions):
    f32, bf16 = jnp.float32, jnp.bfloat16
    length, units = slope.shape
    width, chunk, wide = cot.shape[1], length // 4, 256

    def kernel(*refs):
        (cot, w, slope, att, qkv, log_total, cosine, sine, down, along) = refs[:10]
        (dpre, dqkv, sum_fc1, sum_qkv, sum_cot, datt, dk, dv) = refs[10:]
        total = jnp.zeros((1, width), f32)
        for c in range(4):
            block = cot[c * chunk : (c + 1) * chunk, :].astype(f32)
            total = total + jnp.sum(block, axis=0, keepdims=True)
        sum_cot[...] = total
        datt[...] = mm(cot[...], w[units:, :], NT).astype(bf16)
        for n in range(units // wide):
            here = slice(n * wide, (n + 1) * wide)
            grad = mm(cot[...], w[here, :], NT) * slope[:, here]
            sum_fc1[:, here] = jnp.sum(grad, axis=0, keepdims=True)
            dpre[:, here] = grad.astype(bf16)
        dk[...] = jnp.zeros_like(dk)
        dv[...] = jnp.zeros_like(dv)
        sum_qkv[...] = jnp.zeros_like(sum_qkv)
        for c in range(4):
            here = slice(c * chunk, (c + 1) * chunk)
            queries, grad = qkv[0, here, :], datt[here, :]
            seen = down[here, :] >= along[...]
            scores = mm(queries, qkv[1], NT) * HEAD**-0.5
            prob = jnp.where(seen, jnp.exp(jnp.where(seen, scores, MASKED) - log_total[here, :]), 0.0)
            dot = jnp.sum(grad.astype(f32) * att[here, :].astype(f32), axis=-1, keepdims=True)
            dscore = (prob * (mm(grad, qkv[2], NT) - dot) * HEAD**-0.5).astype(bf16)
            dq = turn(mm(dscore, qkv[1]), cosine[here, :], -sine[here, :])
            sum_qkv[0:1, :] += jnp.sum(dq, axis=0, keepdims=True)
            dqkv[0, here, :] = dq.astype(bf16)
            dk[...] += mm(dscore, queries, TN)
            dv[...] += mm(prob.astype(bf16), grad, TN)
        turned = turn(dk[...], cosine[...], -sine[...])
        sum_qkv[1:2, :] = jnp.sum(turned, axis=0, keepdims=True)
        sum_qkv[2:3, :] = jnp.sum(dv[...], axis=0, keepdims=True)
        dqkv[1] = turned.astype(bf16)
        dqkv[2] = dv[...].astype(bf16)

    args = (cot, w, slope, att, qkv, log_total, *tables, *positions)
    outs = [
        ((length, units), bf16),
        ((3, length, HEAD), bf16),
        ((1, units), f32),
        ((8, HEAD), f32),
        ((1, width), f32),
    ]
    return call(
        kernel,
        (1,),
        [whole(v.shape) for v in args],
        [whole(shape) for shape, _ in outs],
        outs,
        [
            pltpu.VMEM((length, HEAD), bf16),
            pltpu.VMEM((length, HEAD), f32),
            pltpu.VMEM((length, HEAD), f32),
        ],
        args=args,
    )


def input_side(pieces, dpre, dqkv, w_fc1, w_qkv, centre, scale, params):
    f32 = jnp.float32
    count, (piece, width) = len(pieces), pieces[0].shape
    length, units, chunk = count * piece, dpre.shape[1], 512

    def kernel(*refs):
        x = refs[:count]
        dpre, dqkv, w_fc1, w_qkv, centre, scale, par, sums, out, dmlp, dattn = refs[count:]
        dmlp[...] = mm(dpre[...], w_fc1[...], NT)
        dattn[...] = (
            mm(dqkv[0], w_qkv[0], NT) + mm(dqkv[1], w_qkv[1], NT) + mm(dqkv[2], w_qkv[2], NT)
        )
        totals = [jnp.zeros((1, chunk), f32)] * 4
        for r in range(count):
            here = slice(r * piece, (r + 1) * piece)
            normed = (x[r][...].astype(f32) - centre[here, :]) * scale[here, :]
            a, m = dattn[here, :], dmlp[here, :]
            terms = (a * normed, a, m * normed, m)
            totals = [t + jnp.sum(v, axis=0, keepdims=True) for t, v in zip(totals, terms)]
            out[here, :] = (a * par[0:1] + m * par[2:3]).astype(out.dtype)
        for i, total in enumerate(totals):
            sums[i : i + 1, :] = total

    block = pl.BlockSpec((piece, chunk), lambda j: (0, j))
    return call(
        kernel,
        (width // chunk,),
        [block] * count
        + [
            whole(dpre.shape),
            whole(dqkv.shape),
            pl.BlockSpec((chunk, units), lambda j: (j, 0)),
            pl.BlockSpec((3, chunk, HEAD), lambda j: (0, j, 0)),
            whole(centre.shape),
            whole(scale.shape),
            pl.BlockSpec((4, chunk), lambda j: (0, j)),
        ],
        [pl.BlockSpec((rows, chunk), lambda j: (0, j)) for rows in (8, length)],
        [((8, width), f32), ((length, width), jnp.bfloat16)],
        [pltpu.VMEM((length, chunk), f32)] * 2,
        args=(*pieces, dpre, dqkv, w_fc1, w_qkv, centre, scale, params),
    )


def fc1_gradient(mlp_in, dpre, which, arrived=None):
    rows, width = mlp_in[0].shape
    units, chunk = dpre[0].shape[1], 256
    steps = width // 2 // chunk

    def kernel(which, x0, x1, d0, d1, *rest):
        part = mm(x0[...], d0[...], TN) + mm(x1[...], d1[...], TN)
        if arrived is not None:
            part = part + rest[0][...].astype(jnp.float32)
        rest[-1][...] = part.astype(jnp.bfloat16)

    out = pl.BlockSpec((chunk, units), lambda j, _: (j, 0))
    columns = pl.BlockSpec((rows, chunk), lambda j, which: (0, which[0] * steps + j))
    extra = () if arrived is None else (arrived,)
    return call(
        kernel,
        (steps,),
        [columns] * 2 + [whole(dpre[0].shape)] * 2 + [out] * len(extra),
        [out],
        [((width // 2, units), jnp.bfloat16)],
        scalars=(which,),
        args=(*mlp_in, *dpre, *extra),
    )[0]


def send_places_of(spot):
    return [1 - spot[1], 3 - spot[1]]


def keep_places_of(spot):
    return [2 * (1 - spot[0]) + spot[1], 2 * spot[0] + spot[1]]


def rows_gradient(act, att, cot, spot, came=None):
    f32, bf16 = jnp.float32, jnp.bfloat16
    rows, units = act[0].shape
    width, tall, low, chunk = cot[0].shape[1], units // 4, HEAD // 4, 512
    half = len(cot) // 2
    piece = cot[0].shape[0]
    places = send_places_of if came is None else keep_places_of

    def columns(deep):
        return pl.BlockSpec((deep, chunk), lambda j, _: (0, j))

    def stacked(deep):
        return pl.BlockSpec((2, deep, chunk), lambda j, _: (0, 0, j))

    lefts = [
        pl.BlockSpec((rows, tall), lambda j, spot, i=i: (0, places(spot)[i]))
        for i in range(2)
        for _ in range(2)
    ]

    def sending(spot, x0, x1, y0, y1, a0, a1, *refs):
        out, kept, c0, c1, left, head = refs[2 * half :]

        @pl.when(pl.program_id(0) == 0)
        def _():
            for i, pair in enumerate(((x0, x1), (y0, y1), (a0, a1))):
                here = slice(i * tall, (i + 1) * tall)
                left[here, :rows] = pair[0][...].T
                left[here, rows:] = pair[1][...].T

        for i in range(half):
            here = slice(i * piece, (i + 1) * piece)
            c0[here, :] = refs[i][...]
            c1[here, :] = refs[half + i][...]
        for i in range(2):
            part = mm(left[i * tall : (i + 1) * tall, :rows], c0[...])
            part = part + mm(left[i * tall : (i + 1) * tall, rows:], c1[...])
            out[i, :tall, :] = part.astype(bf16)
        head[...] = mm(left[2 * tall :, :rows], c0[...]) + mm(left[2 * tall :, rows:], c1[...])
        for i in range(2):
            q = 2 * i + spot[1]
            out[i, tall:, :] = head[pl.ds(pl.multiple_of((q ^ 1) * low, low), low), :].astype(bf16)
            kept[i] = head[pl.ds(pl.multiple_of(q * low, low), low), :]

    def keeping(spot, x0, x1, y0, y1, c0, c1, came, kept, sent, own, left):
        @pl.when(pl.program_id(0) == 0)
        def _():
            for i, pair in enumerate(((x0, x1), (y0, y1))):
                here = slice(i * tall, (i + 1) * tall)
                left[here, :rows] = pair[0][...].T
                left[here, rows:] = pair[1][...].T

        for i, out in enumerate((sent, own)):
            x = spot[0] ^ (1 - i)
            here = slice(i * tall, (i + 1) * tall)
            part = mm(left[here, :rows], c0[...]) + mm(left[here, rows:], c1[...])
            out[:tall, :] = (part + came[x, :tall, :].astype(f32)).astype(out.dtype)
            out[tall:, :] = (kept[x] + came[x, tall:, :].astype(f32)).astype(out.dtype)

    grid = (width // chunk,)
    if came is None:
        return call(
            sending,
            grid,
            lefts + [whole(v.shape) for v in att] + [columns(piece)] * len(cot),
            [stacked(tall + low), stacked(low), columns(rows), columns(rows)],
            [((2, tall + low, width), bf16), ((2, low, width), f32)] + [((rows, width), bf16)] * 2,
            [pltpu.VMEM((2 * tall + HEAD, 2 * rows), bf16), pltpu.VMEM((HEAD, chunk), f32)],
            scalars=(spot,),
            args=(*act, *act, *att, *cot),
        )
    return call(
        keeping,
        grid,
        lefts + [columns(rows)] * 2 + [stacked(tall + low), stacked(low)],
        [columns(tall + low)] * 2,
        [((tall + low, width), bf16), ((tall + low, width), f32)],
        [pltpu.VMEM((2 * tall, 2 * rows), bf16)],
        scalars=(spot,),
        args=(*act, *act, *cot, *came),
    )


def columns_gradient(attn_in, dqkv, meta, spot, came=None):
    f32, bf16 = jnp.float32, jnp.bfloat16
    rows, width = attn_in[0].shape
    deep, slots = width // 4, meta.shape[0] - 1
    places = send_places_of if came is None else keep_places_of

    lefts = [
        pl.BlockSpec((rows, deep), lambda s, _, spot, i=i: (0, places(spot)[i]))
        for i in range(2)
        for _ in range(2)
    ]
    kind = pl.BlockSpec((1, rows, HEAD), lambda s, meta, _: (meta[1 + s], 0, 0))
    stacked = pl.BlockSpec((2, deep, HEAD), lambda s, *_: (0, 0, s))
    columns = pl.BlockSpec((deep, HEAD), lambda s, *_: (0, s))

    def kernel(meta, spot, x0, x1, y0, y1, d0, d1, *rest):
        left = rest[-1]

        @pl.when(pl.program_id(0) == 0)
        def _():
            for i, pair in enumerate(((x0, x1), (y0, y1))):
                here = slice(i * deep, (i + 1) * deep)
                left[here, :rows] = pair[0][...].T
                left[here, rows:] = pair[1][...].T

        for i in range(2):
            here = slice(i * deep, (i + 1) * deep)
            part = mm(left[here, :rows], d0[0]) + mm(left[here, rows:], d1[0])
            if came is None:
                rest[0][i] = part.astype(bf16)
            else:
                part = part + rest[0][spot[0] ^ (1 - i)].astype(f32)
                rest[1 + i][...] = part.astype(rest[1 + i].dtype)

    if came is None:
        specs, outs, extra = [stacked], [((2, deep, slots * HEAD), bf16)], ()
    else:
        specs, extra = [columns] * 2, (came,)
        outs = [((deep, slots * HEAD), bf16), ((deep, slots * HEAD), f32)]
    return call(
        kernel,
        (slots,),
        lefts + [kind] * 2 + [stacked] * len(extra),
        specs,
        outs,
        [pltpu.VMEM((2 * deep, 2 * rows), bf16)],
        scalars=(meta, spot),
        args=(*attn_in, *attn_in, *dqkv, *extra),
    )


def pack_sums(norm_sums, head_sums, cot_sums, unit_sums, spot):
    f32 = jnp.float32
    width, units = cot_sums[0].shape[1], unit_sums[0].shape[1]
    members = HEADS
    cols = width // members
    begin = 4 * cols + 3 * HEAD
    total = begin + cols + units

    def kernel(spot, n0, n1, h0, h1, c0, c1, u0, u1, mine, sent, rows):
        rows[...] = jnp.zeros_like(rows)
        place = spot[2]
        own = pl.ds(place, 1)
        for m in range(members):
            for i in range(4):
                there = slice(m * cols, (m + 1) * cols)
                rows[m : m + 1, i * cols : (i + 1) * cols] = (
                    n0[i : i + 1, there] + n1[i : i + 1, there]
                )
        for kind in range(3):
            block = kind * HEADS + place
            lanes = pl.ds(pl.multiple_of(4 * cols + block % 3 * HEAD, HEAD), HEAD)
            rows[pl.ds(block // 3, 1), lanes] = h0[kind : kind + 1, :] + h1[kind : kind + 1, :]
        lanes = pl.ds(pl.multiple_of(place * cols, cols), cols)
        rows[own, begin : begin + cols] = c0[:, lanes] + c1[:, lanes]
        rows[own, begin + cols :] = u0[...] + u1[...]
        for z in range(members // 2):
            mine[z : z + 1, :] = rows[pl.ds(2 * z + spot[3], 1), :]
            sent[z : z + 1, :] = rows[pl.ds(2 * z + 1 - spot[3], 1), :]

    args = (*norm_sums, *head_sums, *cot_sums, *unit_sums)
    return call(
        kernel,
        (1,),
        [whole(v.shape) for v in args],
        [whole((members // 2, total))] * 2,
        [((members // 2, total), f32)] * 2,
        [pltpu.VMEM((members, total), f32)],
        scalars=(spot,),
        args=args,
    )


def fold_blocks(partial, arrived, blocks, passing=()):
    f32, bf16 = jnp.float32, jnp.bfloat16
    rows, width = partial.shape
    deep = rows // 4

    def kernel(a, b, *refs):
        more, outs = refs[: len(passing)], refs[len(passing) :]
        for i, (r, out) in enumerate(zip(blocks, outs)):
            here = slice(r * deep, (r + 1) * deep)
            block = a[here, :].astype(f32) + b[here, :].astype(f32)
            if more:
                block = block + more[i][...].astype(f32)
            out[...] = block.astype(out.dtype)

    return call(
        kernel,
        (1,),
        [whole(v.shape) for v in (partial, arrived, *passing)],
        [whole((deep, width))] * len(blocks),
        [((deep, width), bf16 if r else f32) for r in blocks],
        args=(partial, arrived, *passing),
    )


def member_at(spot, k, sign=1):
    return (spot[4] + sign * (k // 2) + HEADS) % (HEADS // 2) * 2 + (spot[3] ^ (k % 2))


def fold_rows(kept, arrived, spot):
    deep, width = kept.shape
    cols = width // HEADS

    def kernel(spot, a, b, *outs):
        for k, out in enumerate(outs):
            here = pl.ds(pl.multiple_of(member_at(spot, k) * cols, cols), cols)
            out[...] = (a[:, here] + b[:, here].astype(jnp.float32)).astype(jnp.bfloat16)

    return call(
        kernel,
        (1,),
        [whole(kept.shape)] * 2,
        [whole((deep, cols))] * HEADS,
        [((deep, cols), jnp.bfloat16)] * HEADS,
        scalars=(spot,),
        args=(kept, arrived),
    )


def pick_rows(w_fc2, w_out, spot):
    cols = w_fc2.shape[1]
    tall, low = w_fc2.shape[0] // HEADS // 4, w_out.shape[0] // HEADS // 4

    def kernel(spot, a, b, *outs):
        for k, out in enumerate(outs):

            @pl.when(pl.program_id(0) == k)
            def _(out=out):
                out[:tall, :] = a[...]
                out[tall:, :] = b[...]

    def block(deep):
        return pl.BlockSpec(
            (deep, cols), lambda k, spot: (4 * member_at(spot, k) + 2 * spot[0] + spot[1], 0)
        )

    return call(
        kernel,
        (HEADS,),
        [block(tall), block(low)],
        [whole((tall + low, cols))] * HEADS,
        [((tall + low, cols), w_fc2.dtype)] * HEADS,
        scalars=(spot,),
        args=(w_fc2, w_out),
    )


def stack_members(pieces, spot):
    shape = pieces[0].shape

    def kernel(spot, *refs):
        for k, ref in enumerate(refs[:-1]):
            refs[-1][member_at(spot, k, -1)] = ref[...]

    return call(
        kernel,
        (1,),
        [whole(shape)] * HEADS,
        [whole((HEADS, *shape))],
        [((HEADS, *shape), pieces[0].dtype)],
        scalars=(spot,),
        args=pieces,
    )[0]


def to_members(pieces):
    ring = lax.axis_size(CTX)
    came = [pieces[0]]
    for k in range(1, len(pieces)):
        route = [
            (2 * z + y, (z + k // 2) % ring * 2 + (y ^ (k % 2))) for z in range(ring) for y in range(2)
        ]
        came.append(lax.ppermute(pieces[k], GROUP, route))
    return came


def fold_slots(kept, arrived, slots):
    deep, width = kept.shape
    cols = width // slots

    def kernel(a, b, *outs):
        for s, out in enumerate(outs):
            here = slice(s * cols, (s + 1) * cols)
            out[...] = (a[:, here] + b[:, here].astype(jnp.float32)).astype(jnp.bfloat16)

    return call(
        kernel,
        (1,),
        [whole(kept.shape)] * 2,
        [whole((deep, cols))] * slots,
        [((deep, cols), jnp.bfloat16)] * slots,
        args=(kept, arrived),
    )


def sum_side(mine, came, spot):
    ring, total = mine.shape

    def kernel(spot, a, b, *refs):
        refs[-1][...] = a[...] + b[...]
        for r, out in enumerate(refs[:-1]):
            out[...] = refs[-1][pl.ds((spot[4] + r) % ring, 1), :]

    return call(
        kernel,
        (1,),
        [whole(mine.shape)] * 2,
        [whole((1, total))] * ring,
        [((1, total), jnp.float32)] * ring,
        [pltpu.VMEM((ring, total), jnp.float32)],
        scalars=(spot,),
        args=(mine, came),
    )


def sum_vectors(mine, sent, spot):
    came = rotated(sent, FSDP, 1)
    total, *rows = sum_side(mine, came, spot)
    for r, row in enumerate(rows, 1):
        total = total + rotated(row, CTX, r)
    total = total + rotated(total, CORE, 1)
    return (total + rotated(total, X, 1))[0]


def spread_columns(pieces, meta):
    deep, wide = pieces[0].shape

    def kernel(meta, p0, p1, p2, p3, out):
        for d, p in enumerate((p0, p1, p2, p3)):

            @pl.when(pl.program_id(0) == d)
            def _(p=p):
                out[...] = p[...].astype(jnp.float32)

    return call(
        kernel,
        (4,),
        [whole((deep, wide))] * 4,
        [pl.BlockSpec((deep, wide), lambda d, meta: (meta[0] ^ d, 0))],
        [((4 * deep, wide), jnp.float32)],
        scalars=(meta,),
        args=pieces,
    )[0]


def spread_rows(pieces, meta):
    members, deep, cols = pieces[0].shape
    low = HEAD // 4
    tall = deep - low

    def kernel(meta, p0, p1, p2, p3, fc2, out):
        for d, p in enumerate((p0, p1, p2, p3)):

            @pl.when(pl.program_id(0) == d)
            def _(p=p):
                for m in range(members):
                    fc2[m, 0] = p[m, :tall, :].astype(jnp.float32)
                    out[m, 0] = p[m, tall:, :].astype(jnp.float32)

    fc2, out = call(
        kernel,
        (4,),
        [whole(pieces[0].shape)] * 4,
        [
            pl.BlockSpec((members, 1, tall, cols), lambda d, meta: (0, meta[0] ^ d, 0, 0)),
            pl.BlockSpec((members, 1, low, cols), lambda d, meta: (0, meta[0] ^ d, 0, 0)),
        ],
        [((members, 4, tall, cols), jnp.float32), ((members, 4, low, cols), jnp.float32)],
        scalars=(meta,),
        args=pieces,
    )
    return fc2.reshape(-1, cols), out.reshape(-1, cols)


def spread_halves(own, twin, spot):
    deep, wide = own[0].shape
    steps = 2

    def kernel(spot, a, b, c, d, out):
        @pl.when(pl.program_id(0) == 0)
        def _():
            out[...] = a[...].astype(jnp.float32) + b[...].astype(jnp.float32)

        @pl.when(pl.program_id(0) == 1)
        def _():
            out[...] = c[...].astype(jnp.float32) + d[...].astype(jnp.float32)

    block = (deep // steps, wide)
    mine = pl.BlockSpec(block, lambda h, j, _: (jnp.where(h == 0, j, steps - 1), 0))
    theirs = pl.BlockSpec(block, lambda h, j, _: (jnp.where(h == 0, 0, j), 0))
    return call(
        kernel,
        (2, steps),
        [mine, mine, theirs, theirs],
        [pl.BlockSpec(block, lambda h, j, spot: ((spot[1] ^ h) * steps + j, 0))],
        [((2 * deep, wide), jnp.float32)],
        scalars=(spot,),
        args=(*own, *twin),
    )[0]


def tensor_layer(*args):
    return group_layer(*args)


def group_layer(
    hidden,
    cotangent,
    ln1_gain,
    ln1_bias,
    ln2_gain,
    ln2_bias,
    w_qkv,
    b_qkv,
    w_out,
    b_out,
    w_fc1,
    b_fc1,
    w_fc2,
    b_fc2,
):
    f32, bf16 = jnp.float32, jnp.bfloat16
    ring = lax.axis_size(CTX)
    members = ring * lax.axis_size(FSDP)
    ctx_at, side = lax.axis_index(CTX), lax.axis_index(FSDP)
    x_at, core_at = lax.axis_index(X), lax.axis_index(CORE)
    place, replica = lax.axis_index(GROUP), lax.axis_index(REPLICAS)
    inputs, upstream_own = hidden[0], cotangent[0]
    row_count, width = inputs.shape
    length = ring * row_count
    cols = width // members
    slots = w_qkv.shape[1] // HEAD

    def quarter(array, dim):
        size = array.shape[dim] // 4
        return lax.dynamic_slice_in_dim(array, replica * size, size, dim)

    hid = gather_line(inputs)
    hid_other = gather_side(hid)
    cot = gather_line(upstream_own)
    cot_other = gather_side(cot)

    kind_of = [[0] * slots for _ in range(members)]
    for block in range(slots * members):
        kind_of[block % members][block % slots] = block // HEADS
    kinds = jnp.asarray(kind_of, jnp.int32)[place]
    meta = jnp.concatenate([replica[None], kinds]).astype(jnp.int32)
    spot = jnp.stack([x_at, core_at, place, side, ctx_at]).astype(jnp.int32)
    token_pos = (
        ((ctx_at - jnp.arange(ring)) % ring)[:, None] * row_count + jnp.arange(row_count)[None]
    ).reshape(length)
    cosine, sine_table = (t[:, 0] for t in rotary_tables(token_pos.astype(f32), ROT))
    rest = ((0, 0), (0, ROPE_LANES - ROT))
    tables = (
        jnp.pad(jnp.concatenate([cosine, cosine], axis=1), rest, constant_values=1.0),
        jnp.pad(jnp.concatenate([-sine_table, sine_table], axis=1), rest),
    )
    positions = (token_pos[:, None], token_pos[None, :])
    b_fc1 = b_fc1.astype(f32)[None]
    twin_core, own_core = (1 - core_at)[None], core_at[None]
    vector = (ln1_gain, ln1_bias, ln2_gain, ln2_bias, b_out, b_fc2, b_qkv)
    vector, meta, spot, tables, positions, b_fc1, twin_core, own_core = lax.optimization_barrier(
        (vector, meta, spot, tables, positions, b_fc1, twin_core, own_core)
    )
    vector = pack_columns([v[None] for v in vector])[0]
    vectors = [vector]
    for r in range(1, ring):
        vectors.append(rotated(vector, CTX, r))
    vectors = jnp.stack(vectors)
    came = rotated(vectors, FSDP, 1)
    both = jnp.stack([vectors, came])
    both = both[jnp.arange(2) ^ side]
    small = jnp.transpose(both[:, (ctx_at - jnp.arange(ring)) % ring], (1, 0, 2))
    small = small.reshape(members, -1).astype(f32)
    gain_one, shift_one, gain_two, shift_two, full_bout, full_bfc2 = (
        small[:, i * cols : (i + 1) * cols].reshape(width) for i in range(6)
    )
    params = jnp.stack([gain_one, shift_one, gain_two, shift_two])
    bias_qkv = small[:, 6 * cols :].reshape(3, HEADS, HEAD)
    bias_qkv = lax.dynamic_slice_in_dim(bias_qkv, place, 1, 1)

    qkv_quarter = quarter(w_qkv, 0)
    moved_columns = []
    for s in range(slots):
        moved_columns.append(
            lax.ppermute(
                qkv_quarter[:, s * HEAD : (s + 1) * HEAD],
                GROUP,
                [(i, (slots * i + s) % members) for i in range(members)],
            )
        )
    moved_columns = pack_columns(moved_columns)

    def replicas(own):
        over_x = rotated(own, X, 1)
        twin = rotated(own, CORE, 1)
        return [own, twin, over_x, rotated(over_x, CORE, 1)]

    head_columns = replicas(moved_columns)
    picked = pick_rows(w_fc2, w_out, spot)
    picked = to_members(picked)
    moved_rows = stack_members(picked, spot)
    row_pieces = replicas(moved_rows)

    rows = (hid, hid_other)
    normed = []
    for i in range(2):
        normed.append(norm_fc1(rows[i], params, w_fc1, b_fc1))
    attn_in, mlp_in, centre, scale, act, slope = zip(*normed)
    head_qkv, *first = head_attention(attn_in[0], head_columns, bias_qkv, tables, positions, meta)
    second = head_attention(attn_in[1], [head_qkv], bias_qkv, tables, positions, meta)
    qkv, attended, log_total = zip(first, second)

    def send_places(partial, arrived):
        own, far = fold_blocks(partial, arrived, (0, 2))
        up = lax.ppermute(far, CTX, [(0, 1), (1, 2)])
        down = lax.ppermute(far, CTX, [(2, 1), (3, 2)])
        low, high = fold_blocks(partial, arrived, (1, 3), (down, up))
        low = rotated(low, CTX, -1)
        high = rotated(high, CTX, -3)
        return [own, low, high]

    row_weights, branch_other = project_other(row_pieces, act[1], attended[1], meta)
    out_y = gather_side([branch_other])[0]
    branch = project_own(row_weights, act[0], attended[0])
    out_z = send_places(branch, out_y)

    row_part, row_kept, *upstream = rows_gradient(act, attended, cot + cot_other, spot)
    backs, inner = [None, None], [None, None]
    for i in (1, 0):
        backs[i] = backward(
            upstream[i], row_weights, slope[i], attended[i], qkv[i], log_total[i], tables, positions
        )
        inner[i] = input_side(
            rows[i],
            backs[i][0],
            backs[i][1],
            w_fc1,
            head_qkv,
            centre[i],
            scale[i],
            params,
        )
    d_preact, d_qkv, sum_fc1, sum_qkv, sum_cot = zip(*backs)
    u_y = gather_side(inner[1][1:])[0]
    u_z = send_places(inner[0][1], u_y)

    row_part = rotated(row_part, CORE, 1)
    row_sent, row_keep = rows_gradient(act, None, upstream, spot, (row_part, row_kept))
    row_sent = rotated(row_sent, X, 1)
    col_part = columns_gradient(attn_in, d_qkv, meta, spot)[0]
    col_part = rotated(col_part, CORE, 1)
    col_sent, col_keep = columns_gradient(attn_in, d_qkv, meta, spot, col_part)
    col_sent = rotated(col_sent, X, 1)
    fc1_part = fc1_gradient(mlp_in, d_preact, twin_core)
    fc1_part = rotated(fc1_part, CORE, 1)
    fc1_half = fc1_gradient(mlp_in, d_preact, own_core, fc1_part)
    fc1_sent = rotated(fc1_half, X, 1)
    fc1_twin = rotated(fc1_half, CORE, 1)
    fc1_both = rotated(fc1_sent, CORE, 1)

    vectors = pack_sums((inner[0][0], inner[1][0]), sum_qkv, sum_cot, sum_fc1, spot)
    vectors = sum_vectors(*vectors, spot)
    g1, s1, g2, s2 = (vectors[i * cols : (i + 1) * cols] for i in range(4))
    bqkv_grad, bout_grad, bfc1_grad = jnp.split(
        vectors[4 * cols :], (slots * HEAD, slots * HEAD + cols)
    )

    col_part = fold_slots(col_keep, col_sent, slots)
    col_back = []
    for s in range(slots):
        col_back.append(
            lax.ppermute(
                col_part[s],
                GROUP,
                [((slots * i + s) % members, i) for i in range(members)],
            )
        )
    row_part = fold_rows(row_keep, row_sent, spot)
    row_part = to_members(row_part)
    row_back = stack_members(row_part, spot)
    fc1_grad = spread_halves((fc1_half, fc1_sent), (fc1_twin, fc1_both), spot)
    col_back = pack_columns(col_back)
    col_back = replicas(col_back)
    qkv_grad = spread_columns(col_back, meta)
    row_back = replicas(row_back)
    fc2_grad, out_grad = spread_rows(row_back, meta)

    own_f = inputs.astype(f32)
    branch = sum(v.astype(f32) for v in out_z)
    output = (own_f + (branch + full_bout + full_bfc2)).astype(bf16)
    merged = sum(v.astype(f32) for v in u_z)
    own_normed, own_std = normalize(own_f)
    input_grad = (
        upstream_own.astype(f32) + norm_backward(merged, own_normed, own_std)
    ).astype(bf16)

    return (
        output[None],
        input_grad[None],
        g1,
        s1,
        g2,
        s2,
        qkv_grad,
        bqkv_grad,
        out_grad,
        bout_grad,
        fc1_grad,
        bfc1_grad,
        fc2_grad,
        bout_grad,
    )


def solution(mesh):
    sizes = dict(mesh.shape)
    fits = (sizes[CTX], sizes[FSDP], sizes[DP]) == (HEADS // 2, 2, 4)
    if fits:
        mesh = Mesh(
            mesh.devices.reshape(2, 2, sizes[CTX], sizes[FSDP]),
            (X, CORE, CTX, FSDP),
        )
    rows = P((*(REPLICAS if fits else (DP,)), FSDP), CTX, None)
    vector, matrix = P(GROUP), P(None, GROUP)
    params = (vector,) * 4 + (matrix, vector) * 4
    return jax.shard_map(
        tensor_layer if fits else plain_layer,
        mesh=mesh,
        in_specs=(rows, rows, *params),
        out_specs=(rows, rows, *params),
        check_vma=False,
    )
```

```python
import math

import jax
import jax.numpy as jnp
from jax import lax
from jax.experimental import pallas as pl
from jax.experimental.pallas import tpu as pltpu
from jax.sharding import Mesh
from jax.sharding import PartitionSpec as P

HEADS = 8
HEAD = 256
ROT = 64


EPSILON = 1e-05
SQRT_HALF = 0.7071067811865476
INV_ROOT_TWO_PI = 0.3989422804014327
MASKED = -1e30

DP, CTX, FSDP, X, CORE = "dp", "ctx", "fsdp", "x", "core"
GROUP, REPLICAS = (CTX, FSDP), (X, CORE)
QK, KV, QT = "qhd,khd->hqk", "hqk,khd->qhd", "hqk,qhd->khd"


def from_behind(value, axis, steps):
    count = lax.axis_size(axis)
    pairs = [(source, (source + steps) % count) for source in range(count)]
    return lax.ppermute(value, axis, pairs)


def shifted(block, axis, distance):
    devices = range(lax.axis_size(axis))
    route = [(i - distance, i) for i in devices if i - distance in devices]
    return lax.ppermute(block, axis, route)


def normalize(inputs):
    centre = jnp.mean(inputs, axis=-1, keepdims=True)
    centred = inputs - centre
    variance = jnp.mean(centred * centred, axis=-1, keepdims=True)
    inv_std = lax.rsqrt(variance + EPSILON)
    return (centred * inv_std, inv_std)


def norm_backward(upstream, normed, inv_std):
    first_mean = jnp.mean(upstream, axis=-1, keepdims=True)
    second_mean = jnp.mean(upstream * normed, axis=-1, keepdims=True)
    return inv_std * (upstream - first_mean - normed * second_mean)


def gelu_parts(preact):
    normal_cdf = 0.5 * (1.0 + lax.erf(preact * SQRT_HALF))
    normal_pdf = jnp.exp(-0.5 * preact * preact) * INV_ROOT_TWO_PI
    return (preact * normal_cdf, normal_cdf + preact * normal_pdf)


def rotary_tables(positions, rot_dims):
    half_dims = rot_dims // 2
    frequency = jnp.exp(
        jnp.arange(half_dims).astype(jnp.float32) * (-2.0 * math.log(10000.0) / rot_dims)
    )
    angles = positions[:, None] * frequency[None, :]
    return (jnp.cos(angles)[:, None, :], jnp.sin(angles)[:, None, :])


def rotate(tensor, cosine, sine_table, rot_dims):
    half_dims = rot_dims // 2
    leading = tensor[..., :half_dims]
    trailing = tensor[..., half_dims:rot_dims]
    return jnp.concatenate(
        [
            leading * cosine - trailing * sine_table,
            trailing * cosine + leading * sine_table,
            tensor[..., rot_dims:],
        ],
        axis=-1,
    )


def contract_rows(left, right):
    return lax.dot_general(
        left, right, (((0,), (0,)), ((), ())), preferred_element_type=jnp.float32
    )


def contract_cols(left, right):
    return lax.dot_general(
        left, right, (((1,), (1,)), ((), ())), preferred_element_type=jnp.float32
    )


def plain_layer(
    hidden,
    cotangent,
    ln1_gain,
    ln1_bias,
    ln2_gain,
    ln2_bias,
    w_qkv,
    b_qkv,
    w_out,
    b_out,
    w_fc1,
    b_fc1,
    w_fc2,
    b_fc2,
):
    inputs = hidden[0]
    upstream_bf = cotangent[0]
    row_count = inputs.shape[0]
    score_scale = HEAD ** (-0.5)
    cycle_size = lax.axis_size(CTX)
    cycle_place = lax.axis_index(CTX)
    attn_gathered = (
        lax.all_gather(ln1_gain, GROUP, axis=0, tiled=True),
        lax.all_gather(ln1_bias, GROUP, axis=0, tiled=True),
        lax.all_gather(w_qkv, GROUP, axis=1, tiled=True),
        lax.all_gather(b_qkv, GROUP, axis=0, tiled=True),
        lax.all_gather(w_out, GROUP, axis=1, tiled=True),
        lax.all_gather(b_out, GROUP, axis=0, tiled=True),
    )
    mlp_gathered = (
        lax.all_gather(ln2_gain, GROUP, axis=0, tiled=True),
        lax.all_gather(ln2_bias, GROUP, axis=0, tiled=True),
        lax.all_gather(w_fc1, GROUP, axis=1, tiled=True),
        lax.all_gather(b_fc1, GROUP, axis=0, tiled=True),
        lax.all_gather(w_fc2, GROUP, axis=1, tiled=True),
        lax.all_gather(b_fc2, GROUP, axis=0, tiled=True),
    )
    gain_one, shift_one, full_qkv, full_bqkv, full_out, full_bout = attn_gathered
    gain_two, shift_two, full_fc1, full_bfc1, full_fc2, full_bfc2 = mlp_gathered
    inputs_f = inputs.astype(jnp.float32)
    normed, inv_std = normalize(inputs_f)
    attn_in = (normed * gain_one.astype(jnp.float32) + shift_one.astype(jnp.float32)).astype(
        jnp.bfloat16
    )
    mlp_in = (normed * gain_two.astype(jnp.float32) + shift_two.astype(jnp.float32)).astype(
        jnp.bfloat16
    )
    joined = jnp.dot(attn_in, full_qkv, preferred_element_type=jnp.float32) + full_bqkv.astype(
        jnp.float32
    )
    joined = joined.reshape(row_count, 3, HEADS, HEAD)
    token_pos = cycle_place * row_count + jnp.arange(row_count, dtype=jnp.int32)
    cosine, sine_table = rotary_tables(token_pos.astype(jnp.float32), ROT)
    queries = rotate(joined[:, 0], cosine, sine_table, ROT).astype(jnp.bfloat16)
    keys_own = rotate(joined[:, 1], cosine, sine_table, ROT).astype(jnp.bfloat16)
    values_own = joined[:, 2].astype(jnp.bfloat16)
    row_top = jnp.full((HEADS, row_count), MASKED, jnp.float32)
    absorb_key_block = lax.all_gather(keys_own, CTX, axis=0, tiled=True)
    absorb_value_block = lax.all_gather(values_own, CTX, axis=0, tiled=True)
    absorb_key_pos = jnp.arange(absorb_key_block.shape[0], dtype=jnp.int32)
    absorb_visible = (token_pos[:, None] >= absorb_key_pos[None, :])[None]
    absorb_scores = (
        jnp.einsum(QK, queries, absorb_key_block, preferred_element_type=jnp.float32)
        * score_scale
    )
    absorb_scores = jnp.where(absorb_visible, absorb_scores, MASKED)
    new_top = jnp.maximum(row_top, jnp.max(absorb_scores, axis=-1))
    weights_exp = jnp.where(absorb_visible, jnp.exp(absorb_scores - new_top[:, :, None]), 0.0)
    row_total = jnp.sum(weights_exp, axis=-1)
    mixed = jnp.einsum(
        KV,
        weights_exp.astype(jnp.bfloat16),
        absorb_value_block,
        preferred_element_type=jnp.float32,
    )
    row_top, row_total, mixed = (new_top, row_total, mixed)
    attended = (mixed / jnp.transpose(row_total)[:, :, None]).astype(jnp.bfloat16)
    log_total = row_top + jnp.log(row_total)
    attended_flat = attended.reshape(row_count, HEADS * HEAD)
    branch_attn = jnp.dot(
        attended_flat, full_out, preferred_element_type=jnp.float32
    ) + full_bout.astype(jnp.float32)
    preact = jnp.dot(mlp_in, full_fc1, preferred_element_type=jnp.float32) + full_bfc1.astype(
        jnp.float32
    )
    activated, slope = gelu_parts(preact)
    act_bf = activated.astype(jnp.bfloat16)
    branch_mlp = jnp.dot(act_bf, full_fc2, preferred_element_type=jnp.float32) + full_bfc2.astype(
        jnp.float32
    )
    output = (inputs_f + branch_attn + branch_mlp).astype(jnp.bfloat16)
    rows_all = (
        lax.all_gather(inputs, GROUP, axis=0, tiled=True),
        lax.all_gather(act_bf, GROUP, axis=0, tiled=True),
        lax.all_gather(attended_flat, GROUP, axis=0, tiled=True),
    )
    attn_gathered = (
        lax.all_gather(ln1_gain, GROUP, axis=0, tiled=True),
        lax.all_gather(ln1_bias, GROUP, axis=0, tiled=True),
        lax.all_gather(w_qkv, GROUP, axis=1, tiled=True),
        lax.all_gather(b_qkv, GROUP, axis=0, tiled=True),
        lax.all_gather(w_out, GROUP, axis=1, tiled=True),
        lax.all_gather(b_out, GROUP, axis=0, tiled=True),
    )
    mlp_gathered = (
        lax.all_gather(ln2_gain, GROUP, axis=0, tiled=True),
        lax.all_gather(ln2_bias, GROUP, axis=0, tiled=True),
        lax.all_gather(w_fc1, GROUP, axis=1, tiled=True),
        lax.all_gather(b_fc1, GROUP, axis=0, tiled=True),
        lax.all_gather(w_fc2, GROUP, axis=1, tiled=True),
        lax.all_gather(b_fc2, GROUP, axis=0, tiled=True),
    )
    gain_one, shift_one, full_qkv, full_bqkv, full_out, full_bout = attn_gathered
    gain_two, shift_two, full_fc1, full_bfc1, full_fc2, full_bfc2 = mlp_gathered
    upstream = upstream_bf.astype(jnp.float32)
    bias_out_grad = jnp.sum(upstream, axis=0)
    d_act = contract_cols(upstream_bf, full_fc2)
    d_preact = d_act * slope
    d_preact_bf = d_preact.astype(jnp.bfloat16)
    d_mlp_in = contract_cols(d_preact_bf, full_fc1)
    fc1_bias_grad = jnp.sum(d_preact, axis=0)
    ln2_gain_part = jnp.sum(d_mlp_in * normed, axis=0)
    ln2_bias_part = jnp.sum(d_mlp_in, axis=0)
    d_attended = (
        contract_cols(upstream_bf, full_out).astype(jnp.bfloat16).reshape(row_count, HEADS, HEAD)
    )
    row_dot = jnp.transpose(
        jnp.sum(d_attended.astype(jnp.float32) * attended.astype(jnp.float32), axis=-1)
    )
    d_queries = jnp.zeros((row_count, HEADS, HEAD), jnp.float32)
    travelling = (keys_own, values_own)
    key_grads = (
        jnp.zeros((row_count, HEADS, HEAD), jnp.float32),
        jnp.zeros((row_count, HEADS, HEAD), jnp.float32),
    )
    for turn_index in range(cycle_size):
        source = (cycle_place - turn_index) % cycle_size
        key_pos = source * row_count + jnp.arange(row_count, dtype=jnp.int32)
        key_block, value_block = travelling
        visible = (token_pos[:, None] >= key_pos[None, :])[None]
        scores = (
            jnp.einsum(QK, queries, key_block, preferred_element_type=jnp.float32)
            * score_scale
        )
        scores = jnp.where(visible, scores, MASKED)
        probability = jnp.where(visible, jnp.exp(scores - log_total[:, :, None]), 0.0)
        d_probability = jnp.einsum(
            QK, d_attended, value_block, preferred_element_type=jnp.float32
        )
        d_scores = (probability * (d_probability - row_dot[:, :, None]) * score_scale).astype(
            jnp.bfloat16
        )
        d_queries = d_queries + jnp.einsum(
            KV, d_scores, key_block, preferred_element_type=jnp.float32
        )
        key_grads = (
            key_grads[0]
            + jnp.einsum(QT, d_scores, queries, preferred_element_type=jnp.float32),
            key_grads[1]
            + jnp.einsum(
                QT,
                probability.astype(jnp.bfloat16),
                d_attended,
                preferred_element_type=jnp.float32,
            ),
        )
        key_grads = from_behind((key_grads[0], key_grads[1]), CTX, 1)
        if turn_index + 1 < cycle_size:
            travelling = shifted((travelling[0], travelling[1]), CTX, 1)
    d_queries = rotate(d_queries, cosine, -sine_table, ROT)
    d_keys = rotate(key_grads[0], cosine, -sine_table, ROT)
    d_joined = jnp.stack([d_queries, d_keys, key_grads[1]], axis=1).reshape(
        row_count, 3 * HEADS * HEAD
    )
    d_joined_bf = d_joined.astype(jnp.bfloat16)
    d_attn_in = contract_cols(d_joined_bf, full_qkv)
    qkv_bias_grad = jnp.sum(d_joined, axis=0)
    ln1_gain_part = jnp.sum(d_attn_in * normed, axis=0)
    ln1_bias_part = jnp.sum(d_attn_in, axis=0)
    columns = (
        lax.all_to_all(upstream_bf, GROUP, split_axis=1, concat_axis=0, tiled=True),
        lax.all_to_all(d_preact_bf, GROUP, split_axis=1, concat_axis=0, tiled=True),
        lax.all_to_all(d_joined_bf, GROUP, split_axis=1, concat_axis=0, tiled=True),
    )
    small = (
        lax.psum_scatter(ln1_gain_part, GROUP, scatter_dimension=0, tiled=True),
        lax.psum_scatter(ln1_bias_part, GROUP, scatter_dimension=0, tiled=True),
        lax.psum_scatter(ln2_gain_part, GROUP, scatter_dimension=0, tiled=True),
        lax.psum_scatter(ln2_bias_part, GROUP, scatter_dimension=0, tiled=True),
        lax.psum_scatter(qkv_bias_grad, GROUP, scatter_dimension=0, tiled=True),
        lax.psum_scatter(bias_out_grad, GROUP, scatter_dimension=0, tiled=True),
        lax.psum_scatter(fc1_bias_grad, GROUP, scatter_dimension=0, tiled=True),
    )
    normed_all, _ = normalize(rows_all[0].astype(jnp.float32))
    attn_all = (normed_all * gain_one.astype(jnp.float32) + shift_one.astype(jnp.float32)).astype(
        jnp.bfloat16
    )
    mlp_all = (normed_all * gain_two.astype(jnp.float32) + shift_two.astype(jnp.float32)).astype(
        jnp.bfloat16
    )
    fc2_part = contract_rows(rows_all[1], columns[0])
    out_part = contract_rows(rows_all[2], columns[0])
    fc1_part = contract_rows(mlp_all, columns[1])
    qkv_part = contract_rows(attn_all, columns[2])
    owned = (
        small[0],
        small[1],
        small[2],
        small[3],
        qkv_part,
        small[4],
        out_part,
        small[5],
        fc1_part,
        small[6],
        fc2_part,
    )
    merged = d_attn_in * gain_one.astype(jnp.float32) + d_mlp_in * gain_two.astype(jnp.float32)
    input_grad = (upstream + norm_backward(merged, normed, inv_std)).astype(jnp.bfloat16)
    totals = lax.psum(
        (
            owned[0],
            owned[1],
            owned[2],
            owned[3],
            owned[4],
            owned[5],
            owned[6],
            owned[7],
            owned[8],
            owned[9],
            owned[10],
        ),
        DP,
    )
    return (
        output[None],
        input_grad[None],
        totals[0],
        totals[1],
        totals[2],
        totals[3],
        totals[4],
        totals[5],
        totals[6],
        totals[7],
        totals[8],
        totals[9],
        totals[10],
        totals[7],
    )


def rotated(value, axis, steps):
    count = lax.axis_size(axis)
    return lax.ppermute(value, axis, [(i, (i + steps) % count) for i in range(count)])


def gather_line(block):
    place = lax.axis_index(CTX)
    low = rotated(block, CTX, 1)
    high = rotated(block, CTX, 3)
    up = lax.ppermute(low, CTX, [(1, 2), (2, 3)])
    down = lax.ppermute(high, CTX, [(2, 1), (1, 0)])
    middle = jnp.where(place >= 2, up, down)
    return [block, low, middle, high]


def gather_side(blocks):
    gathered = []
    for block in blocks:
        gathered.append(rotated(block, FSDP, 1))
    return gathered


NT = (((1,), (1,)), ((), ()))
TN = (((0,), (0,)), ((), ()))
NN = (((1,), (0,)), ((), ()))
ROPE_LANES = 128
VMEM_LIMIT = 16 << 20


def mm(left, right, dims=NN):
    return lax.dot_general(left, right, dims, preferred_element_type=jnp.float32)


def whole(shape):
    return pl.BlockSpec(shape, lambda *_: (0,) * len(shape), pipeline_mode=pl.Buffered(1))


def call(kernel, grid, in_specs, out_specs, outs, scratch=(), scalars=(), args=()):
    return pl.pallas_call(
        kernel,
        grid_spec=pltpu.PrefetchScalarGridSpec(
            num_scalar_prefetch=len(scalars),
            grid=grid,
            in_specs=in_specs,
            out_specs=out_specs,
            scratch_shapes=list(scratch),
        ),
        out_shape=[jax.ShapeDtypeStruct(shape, dtype) for shape, dtype in outs],
        compiler_params=pltpu.CompilerParams(vmem_limit_bytes=VMEM_LIMIT),
    )(*scalars, *args)


def pack_columns(pieces):
    rows = pieces[0].shape[0]
    total = sum(p.shape[1] for p in pieces)

    def kernel(*refs):
        begin = 0
        for ref in refs[:-1]:
            end = begin + ref.shape[1]
            refs[-1][:, begin:end] = ref[...]
            begin = end

    return call(
        kernel,
        (1,),
        [whole(p.shape) for p in pieces],
        [whole((rows, total))],
        [((rows, total), pieces[0].dtype)],
        args=pieces,
    )[0]


def norm_fc1(pieces, params, w_fc1, b_fc1):
    f32, bf16 = jnp.float32, jnp.bfloat16
    count, (piece, width) = len(pieces), pieces[0].shape
    rows, units = count * piece, w_fc1.shape[1]
    chunk, step, tall = 256, 64, 256

    def kernel(*refs):
        piece_refs, (par, w, b, attn, mlp, centre, scale, act, slope) = refs[:count], refs[count:]

        @pl.when(pl.program_id(0) == 0)
        def _():
            for i in range(count):

                def norm(k, _, i=i):
                    x = piece_refs[i][pl.ds(pl.multiple_of(k * step, step), step), :].astype(f32)
                    mean = jnp.mean(x, axis=-1, keepdims=True)
                    x = x - mean
                    inv = lax.rsqrt(jnp.mean(x * x, axis=-1, keepdims=True) + EPSILON)
                    x = x * inv
                    here = pl.ds(pl.multiple_of(i * piece + k * step, step), step)
                    attn[here, :] = (x * par[0:1] + par[1:2]).astype(bf16)
                    mlp[here, :] = (x * par[2:3] + par[3:4]).astype(bf16)
                    centre[here, :] = mean
                    scale[here, :] = inv
                    return 0

                lax.fori_loop(0, piece // step, norm, 0)

        for r in range(rows // tall):
            here = slice(r * tall, (r + 1) * tall)
            activated, gradient = gelu_parts(mm(mlp[here, :], w[...]) + b[...])
            act[here, :] = activated.astype(bf16)
            slope[here, :] = gradient

    column = pl.BlockSpec((rows, chunk), lambda j: (0, j))
    return call(
        kernel,
        (units // chunk,),
        [whole((piece, width))] * count
        + [
            whole(params.shape),
            pl.BlockSpec((width, chunk), lambda j: (0, j)),
            pl.BlockSpec((1, chunk), lambda j: (0, j)),
        ],
        [whole((rows, width))] * 2 + [whole((rows, 1))] * 2 + [column] * 2,
        [((rows, width), bf16)] * 2
        + [((rows, 1), f32)] * 2
        + [((rows, units), bf16), ((rows, units), f32)],
        args=(*pieces, params, w_fc1, b_fc1),
    )


def turn(tensor, cosine, sine):
    first = tensor[:, :ROPE_LANES]
    lane = lax.broadcasted_iota(jnp.int32, first.shape, 1)
    swapped = jnp.where(
        lane < ROT // 2,
        pltpu.roll(first, ROPE_LANES - ROT // 2, 1),
        pltpu.roll(first, ROT // 2, 1),
    )
    return jnp.concatenate([first * cosine + swapped * sine, tensor[:, ROPE_LANES:]], axis=1)


def seen_by(spot, block, rows, length):
    ring = length // rows
    first = (spot[4] - block + ring) % ring * rows
    lane = lax.broadcasted_iota(jnp.int32, (1, length), 1)
    keys = (spot[4] - lane // rows + ring) % ring * rows + lane % rows
    return first + lax.broadcasted_iota(jnp.int32, (rows, 1), 0) >= keys


def join_columns(pieces, meta):
    deep, slots = pieces[0].shape[0], pieces[0].shape[1] // HEAD

    def kernel(meta, p0, p1, p2, p3, w):
        for d, p in enumerate((p0, p1, p2, p3)):
            here = pl.ds(pl.multiple_of((meta[0] ^ d) * deep, deep), deep)
            for s in range(slots):
                w[meta[1 + s], here, :] = p[:, s * HEAD : (s + 1) * HEAD]

    shape = (slots, 4 * deep, HEAD)
    return call(
        kernel,
        (1,),
        [whole(p.shape) for p in pieces],
        [whole(shape)],
        [(shape, pieces[0].dtype)],
        scalars=(meta,),
        args=pieces,
    )[0]


def head_attention(attn_in, weights, bias, tables, spot):
    f32, bf16 = jnp.float32, jnp.bfloat16
    length = attn_in.shape[0]
    chunk = length // 4

    def kernel(spot, x, w, b, cosine, sine, qkv, att, log_total):
        for kind in range(3):
            t = mm(x[...], w[kind]) + b[kind]
            if kind < 2:
                t = turn(t, cosine[...], sine[...])
            qkv[kind] = t.astype(bf16)

        def attend(c, _):
            here = pl.ds(pl.multiple_of(c * chunk, chunk), chunk)
            seen = seen_by(spot, c, chunk, length)
            scores = jnp.where(seen, mm(qkv[0, here, :], qkv[1], NT) * HEAD**-0.5, MASKED)
            top = jnp.max(scores, axis=-1, keepdims=True)
            powers = jnp.where(seen, jnp.exp(scores - top), 0.0)
            total = jnp.sum(powers, axis=-1, keepdims=True)
            att[here, :] = (mm(powers.astype(bf16), qkv[2]) / total).astype(bf16)
            log_total[here, :] = top + jnp.log(total)
            return 0

        lax.fori_loop(0, spot[5], attend, 0)

    args = (attn_in, weights, bias, *tables)
    outs = [((3, length, HEAD), bf16), ((length, HEAD), bf16), ((length, 1), f32)]
    return call(
        kernel,
        (1,),
        [whole(v.shape) for v in args],
        [whole(shape) for shape, _ in outs],
        outs,
        scalars=(spot,),
        args=args,
    )


def project_other(pieces, act, att, meta):
    bf16 = jnp.bfloat16
    members, _, cols = pieces[0].shape
    length, units = act.shape
    width = members * cols
    tall, low = units // 4, HEAD // 4

    def kernel(meta, p0, p1, p2, p3, act, att, w, out):
        for d, p in enumerate((p0, p1, p2, p3)):
            q = meta[0] ^ d
            upper = pl.ds(pl.multiple_of(q * tall, tall), tall)
            lower = pl.ds(pl.multiple_of(units + q * low, low), low)
            for m in range(members):
                w[upper, m * cols : (m + 1) * cols] = p[m, :tall, :]
                w[lower, m * cols : (m + 1) * cols] = p[m, tall:, :]

        def columns(m, _):
            here = pl.ds(pl.multiple_of(m * 2 * cols, 2 * cols), 2 * cols)
            part = mm(act[...], w[:units, here]) + mm(att[...], w[units:, here])
            out[:, here] = part.astype(bf16)
            return 0

        lax.fori_loop(0, members // 2, columns, 0)

    args = (*pieces, act, att)
    return call(
        kernel,
        (1,),
        [whole(v.shape) for v in args],
        [whole((units + HEAD, width)), whole((length, width))],
        [((units + HEAD, width), bf16), ((length, width), bf16)],
        scalars=(meta,),
        args=args,
    )


def project_own(w, act, att):
    length, units = act.shape
    width, chunk = w.shape[1], 512

    def kernel(w, act, att, out, both):
        @pl.when(pl.program_id(0) == 0)
        def _():
            both[:, :units] = act[...]
            both[:, units:] = att[...]

        out[...] = mm(both[...], w[...]).astype(out.dtype)

    return call(
        kernel,
        (width // chunk,),
        [pl.BlockSpec((units + HEAD, chunk), lambda j: (0, j)), whole(act.shape), whole(att.shape)],
        [pl.BlockSpec((length, chunk), lambda j: (0, j))],
        [((length, width), jnp.bfloat16)],
        [pltpu.VMEM((length, units + HEAD), jnp.bfloat16)],
        args=(w, act, att),
    )[0]


def backward(cot, w, slope, att, qkv, log_total, tables, spot):
    f32, bf16 = jnp.float32, jnp.bfloat16
    length, units = slope.shape
    width, chunk, wide = cot.shape[1], length // 4, 256

    def kernel(spot, *refs):
        (cot, w, slope, att, qkv, log_total, cosine, sine) = refs[:8]
        (dpre, dqkv, sum_fc1, sum_qkv, sum_cot, datt, dk, dv) = refs[8:]
        sum_cot[...] = jnp.zeros_like(sum_cot)

        def count(c, _):
            here = pl.ds(pl.multiple_of(c * chunk, chunk), chunk)
            sum_cot[...] += jnp.sum(cot[here, :].astype(f32), axis=0, keepdims=True)
            return 0

        lax.fori_loop(0, spot[5], count, 0)
        datt[...] = mm(cot[...], w[units:, :], NT).astype(bf16)
        for n in range(units // wide):
            here = slice(n * wide, (n + 1) * wide)
            grad = mm(cot[...], w[here, :], NT) * slope[:, here]
            sum_fc1[:, here] = jnp.sum(grad, axis=0, keepdims=True)
            dpre[:, here] = grad.astype(bf16)
        dk[...] = jnp.zeros_like(dk)
        dv[...] = jnp.zeros_like(dv)
        sum_qkv[...] = jnp.zeros_like(sum_qkv)
        for c in range(4):
            here = slice(c * chunk, (c + 1) * chunk)
            queries, grad = qkv[0, here, :], datt[here, :]
            seen = seen_by(spot, c, chunk, length)
            scores = mm(queries, qkv[1], NT) * HEAD**-0.5
            prob = jnp.where(seen, jnp.exp(jnp.where(seen, scores, MASKED) - log_total[here, :]), 0.0)
            dot = jnp.sum(grad.astype(f32) * att[here, :].astype(f32), axis=-1, keepdims=True)
            dscore = (prob * (mm(grad, qkv[2], NT) - dot) * HEAD**-0.5).astype(bf16)
            dq = turn(mm(dscore, qkv[1]), cosine[here, :], -sine[here, :])
            sum_qkv[0:1, :] += jnp.sum(dq, axis=0, keepdims=True)
            dqkv[0, here, :] = dq.astype(bf16)
            dk[...] += mm(dscore, queries, TN)
            dv[...] += mm(prob.astype(bf16), grad, TN)
        turned = turn(dk[...], cosine[...], -sine[...])
        sum_qkv[1:2, :] = jnp.sum(turned, axis=0, keepdims=True)
        sum_qkv[2:3, :] = jnp.sum(dv[...], axis=0, keepdims=True)
        dqkv[1] = turned.astype(bf16)
        dqkv[2] = dv[...].astype(bf16)

    args = (cot, w, slope, att, qkv, log_total, *tables)
    outs = [
        ((length, units), bf16),
        ((3, length, HEAD), bf16),
        ((1, units), f32),
        ((8, HEAD), f32),
        ((1, width), f32),
    ]
    return call(
        kernel,
        (1,),
        [whole(v.shape) for v in args],
        [whole(shape) for shape, _ in outs],
        outs,
        [
            pltpu.VMEM((length, HEAD), bf16),
            pltpu.VMEM((length, HEAD), f32),
            pltpu.VMEM((length, HEAD), f32),
        ],
        scalars=(spot,),
        args=args,
    )


def input_side(pieces, dpre, dqkv, w_fc1, w_qkv, centre, scale, params):
    f32 = jnp.float32
    count, (piece, width) = len(pieces), pieces[0].shape
    length, units, chunk = count * piece, dpre.shape[1], 512

    def kernel(*refs):
        x = refs[:count]
        dpre, dqkv, w_fc1, w_qkv, centre, scale, par, sums, out, dmlp, dattn = refs[count:]
        dmlp[...] = mm(dpre[...], w_fc1[...], NT)
        dattn[...] = (
            mm(dqkv[0], w_qkv[0], NT) + mm(dqkv[1], w_qkv[1], NT) + mm(dqkv[2], w_qkv[2], NT)
        )
        totals = [jnp.zeros((1, chunk), f32)] * 4
        for r in range(count):
            here = slice(r * piece, (r + 1) * piece)
            normed = (x[r][...].astype(f32) - centre[here, :]) * scale[here, :]
            a, m = dattn[here, :], dmlp[here, :]
            terms = (a * normed, a, m * normed, m)
            totals = [t + jnp.sum(v, axis=0, keepdims=True) for t, v in zip(totals, terms)]
            out[here, :] = (a * par[0:1] + m * par[2:3]).astype(out.dtype)
        for i, total in enumerate(totals):
            sums[i : i + 1, :] = total

    block = pl.BlockSpec((piece, chunk), lambda j: (0, j))
    return call(
        kernel,
        (width // chunk,),
        [block] * count
        + [
            whole(dpre.shape),
            whole(dqkv.shape),
            pl.BlockSpec((chunk, units), lambda j: (j, 0)),
            pl.BlockSpec((3, chunk, HEAD), lambda j: (0, j, 0)),
            whole(centre.shape),
            whole(scale.shape),
            pl.BlockSpec((4, chunk), lambda j: (0, j)),
        ],
        [pl.BlockSpec((rows, chunk), lambda j: (0, j)) for rows in (8, length)],
        [((8, width), f32), ((length, width), jnp.bfloat16)],
        [pltpu.VMEM((length, chunk), f32)] * 2,
        args=(*pieces, dpre, dqkv, w_fc1, w_qkv, centre, scale, params),
    )


def fc1_gradient(mlp_in, dpre, which, arrived=None):
    rows, width = mlp_in[0].shape
    units, chunk = dpre[0].shape[1], 256
    steps = width // 2 // chunk

    def kernel(which, x0, x1, d0, d1, *rest):
        part = mm(x0[...], d0[...], TN) + mm(x1[...], d1[...], TN)
        if arrived is not None:
            part = part + rest[0][...].astype(jnp.float32)
        rest[-1][...] = part.astype(jnp.bfloat16)

    out = pl.BlockSpec((chunk, units), lambda j, _: (j, 0))
    columns = pl.BlockSpec((rows, chunk), lambda j, which: (0, which[0] * steps + j))
    extra = () if arrived is None else (arrived,)
    return call(
        kernel,
        (steps,),
        [columns] * 2 + [whole(dpre[0].shape)] * 2 + [out] * len(extra),
        [out],
        [((width // 2, units), jnp.bfloat16)],
        scalars=(which,),
        args=(*mlp_in, *dpre, *extra),
    )[0]


def send_places_of(spot):
    return [1 - spot[1], 3 - spot[1]]


def keep_places_of(spot):
    return [2 * (1 - spot[0]) + spot[1], 2 * spot[0] + spot[1]]


def rows_gradient(act, att, cot, spot, came=None):
    f32, bf16 = jnp.float32, jnp.bfloat16
    rows, units = act[0].shape
    width, tall, low, chunk = cot[0].shape[1], units // 4, HEAD // 4, 512
    half = len(cot) // 2
    piece = cot[0].shape[0]
    places = send_places_of if came is None else keep_places_of

    def columns(deep):
        return pl.BlockSpec((deep, chunk), lambda j, _: (0, j))

    def stacked(deep):
        return pl.BlockSpec((2, deep, chunk), lambda j, _: (0, 0, j))

    lefts = [
        pl.BlockSpec((rows, tall), lambda j, spot, i=i: (0, places(spot)[i]))
        for i in range(2)
        for _ in range(2)
    ]

    def sending(spot, x0, x1, y0, y1, a0, a1, *refs):
        out, kept, c0, c1, left, head = refs[2 * half :]

        @pl.when(pl.program_id(0) == 0)
        def _():
            for i, pair in enumerate(((x0, x1), (y0, y1), (a0, a1))):
                here = slice(i * tall, (i + 1) * tall)
                left[here, :rows] = pair[0][...].T
                left[here, rows:] = pair[1][...].T

        for i in range(half):
            here = slice(i * piece, (i + 1) * piece)
            c0[here, :] = refs[i][...]
            c1[here, :] = refs[half + i][...]
        for i in range(2):
            part = mm(left[i * tall : (i + 1) * tall, :rows], c0[...])
            part = part + mm(left[i * tall : (i + 1) * tall, rows:], c1[...])
            out[i, :tall, :] = part.astype(bf16)
        head[...] = mm(left[2 * tall :, :rows], c0[...]) + mm(left[2 * tall :, rows:], c1[...])
        for i in range(2):
            q = 2 * i + spot[1]
            out[i, tall:, :] = head[pl.ds(pl.multiple_of((q ^ 1) * low, low), low), :].astype(bf16)
            kept[i] = head[pl.ds(pl.multiple_of(q * low, low), low), :]

    def keeping(spot, x0, x1, y0, y1, c0, c1, came, kept, sent, own, left):
        @pl.when(pl.program_id(0) == 0)
        def _():
            for i, pair in enumerate(((x0, x1), (y0, y1))):
                here = slice(i * tall, (i + 1) * tall)
                left[here, :rows] = pair[0][...].T
                left[here, rows:] = pair[1][...].T

        for i, out in enumerate((sent, own)):
            x = spot[0] ^ (1 - i)
            here = slice(i * tall, (i + 1) * tall)
            part = mm(left[here, :rows], c0[...]) + mm(left[here, rows:], c1[...])
            out[:tall, :] = (part + came[x, :tall, :].astype(f32)).astype(out.dtype)
            out[tall:, :] = (kept[x] + came[x, tall:, :].astype(f32)).astype(out.dtype)

    grid = (width // chunk,)
    if came is None:
        return call(
            sending,
            grid,
            lefts + [whole(v.shape) for v in att] + [columns(piece)] * len(cot),
            [stacked(tall + low), stacked(low), columns(rows), columns(rows)],
            [((2, tall + low, width), bf16), ((2, low, width), f32)] + [((rows, width), bf16)] * 2,
            [pltpu.VMEM((2 * tall + HEAD, 2 * rows), bf16), pltpu.VMEM((HEAD, chunk), f32)],
            scalars=(spot,),
            args=(*act, *act, *att, *cot),
        )
    return call(
        keeping,
        grid,
        lefts + [columns(rows)] * 2 + [stacked(tall + low), stacked(low)],
        [columns(tall + low)] * 2,
        [((tall + low, width), bf16), ((tall + low, width), f32)],
        [pltpu.VMEM((2 * tall, 2 * rows), bf16)],
        scalars=(spot,),
        args=(*act, *act, *cot, *came),
    )


def columns_gradient(attn_in, dqkv, meta, spot, came=None):
    f32, bf16 = jnp.float32, jnp.bfloat16
    rows, width = attn_in[0].shape
    deep, slots = width // 4, meta.shape[0] - 1
    places = send_places_of if came is None else keep_places_of

    lefts = [
        pl.BlockSpec((rows, deep), lambda s, _, spot, i=i: (0, places(spot)[i]))
        for i in range(2)
        for _ in range(2)
    ]
    kind = pl.BlockSpec((1, rows, HEAD), lambda s, meta, _: (meta[1 + s], 0, 0))
    stacked = pl.BlockSpec((2, deep, HEAD), lambda s, *_: (0, 0, s))
    columns = pl.BlockSpec((deep, HEAD), lambda s, *_: (0, s))

    def kernel(meta, spot, x0, x1, y0, y1, d0, d1, *rest):
        left = rest[-1]

        @pl.when(pl.program_id(0) == 0)
        def _():
            for i, pair in enumerate(((x0, x1), (y0, y1))):
                here = slice(i * deep, (i + 1) * deep)
                left[here, :rows] = pair[0][...].T
                left[here, rows:] = pair[1][...].T

        for i in range(2):
            here = slice(i * deep, (i + 1) * deep)
            part = mm(left[here, :rows], d0[0]) + mm(left[here, rows:], d1[0])
            if came is None:
                rest[0][i] = part.astype(bf16)
            else:
                part = part + rest[0][spot[0] ^ (1 - i)].astype(f32)
                rest[1 + i][...] = part.astype(rest[1 + i].dtype)

    if came is None:
        specs, outs, extra = [stacked], [((2, deep, slots * HEAD), bf16)], ()
    else:
        specs, extra = [columns] * 2, (came,)
        outs = [((deep, slots * HEAD), bf16), ((deep, slots * HEAD), f32)]
    return call(
        kernel,
        (slots,),
        lefts + [kind] * 2 + [stacked] * len(extra),
        specs,
        outs,
        [pltpu.VMEM((2 * deep, 2 * rows), bf16)],
        scalars=(meta, spot),
        args=(*attn_in, *attn_in, *dqkv, *extra),
    )


def pack_sums(norm_sums, head_sums, cot_sums, unit_sums, spot):
    f32 = jnp.float32
    width, units = cot_sums[0].shape[1], unit_sums[0].shape[1]
    members = HEADS
    cols = width // members
    begin = 4 * cols + 3 * HEAD
    total = begin + cols + units

    def kernel(spot, n0, n1, h0, h1, c0, c1, u0, u1, mine, sent, rows):
        rows[...] = jnp.zeros_like(rows)
        place = spot[2]
        own = pl.ds(place, 1)
        for m in range(members):
            for i in range(4):
                there = slice(m * cols, (m + 1) * cols)
                rows[m : m + 1, i * cols : (i + 1) * cols] = (
                    n0[i : i + 1, there] + n1[i : i + 1, there]
                )
        for kind in range(3):
            block = kind * HEADS + place
            lanes = pl.ds(pl.multiple_of(4 * cols + block % 3 * HEAD, HEAD), HEAD)
            rows[pl.ds(block // 3, 1), lanes] = h0[kind : kind + 1, :] + h1[kind : kind + 1, :]
        lanes = pl.ds(pl.multiple_of(place * cols, cols), cols)
        rows[own, begin : begin + cols] = c0[:, lanes] + c1[:, lanes]
        rows[own, begin + cols :] = u0[...] + u1[...]
        for z in range(members // 2):
            mine[z : z + 1, :] = rows[pl.ds(2 * z + spot[3], 1), :]
            sent[z : z + 1, :] = rows[pl.ds(2 * z + 1 - spot[3], 1), :]

    args = (*norm_sums, *head_sums, *cot_sums, *unit_sums)
    return call(
        kernel,
        (1,),
        [whole(v.shape) for v in args],
        [whole((members // 2, total))] * 2,
        [((members // 2, total), f32)] * 2,
        [pltpu.VMEM((members, total), f32)],
        scalars=(spot,),
        args=args,
    )


def fold_blocks(partial, arrived, blocks, passing=()):
    f32, bf16 = jnp.float32, jnp.bfloat16
    rows, width = partial.shape
    deep = rows // 4

    def kernel(a, b, *refs):
        more, outs = refs[: len(passing)], refs[len(passing) :]
        for i, (r, out) in enumerate(zip(blocks, outs)):
            here = slice(r * deep, (r + 1) * deep)
            block = a[here, :].astype(f32) + b[here, :].astype(f32)
            if more:
                block = block + more[i][...].astype(f32)
            out[...] = block.astype(out.dtype)

    return call(
        kernel,
        (1,),
        [whole(v.shape) for v in (partial, arrived, *passing)],
        [whole((deep, width))] * len(blocks),
        [((deep, width), bf16 if r else f32) for r in blocks],
        args=(partial, arrived, *passing),
    )


def member_at(spot, k, sign=1):
    return (spot[4] + sign * (k // 2) + HEADS) % (HEADS // 2) * 2 + (spot[3] ^ (k % 2))


def fold_rows(kept, arrived, spot):
    deep, width = kept.shape
    cols = width // HEADS

    def kernel(spot, a, b, *outs):
        for k, out in enumerate(outs):
            here = pl.ds(pl.multiple_of(member_at(spot, k) * cols, cols), cols)
            out[...] = (a[:, here] + b[:, here].astype(jnp.float32)).astype(jnp.bfloat16)

    return call(
        kernel,
        (1,),
        [whole(kept.shape)] * 2,
        [whole((deep, cols))] * HEADS,
        [((deep, cols), jnp.bfloat16)] * HEADS,
        scalars=(spot,),
        args=(kept, arrived),
    )


def pick_rows(w_fc2, w_out, spot):
    cols = w_fc2.shape[1]
    tall, low = w_fc2.shape[0] // HEADS // 4, w_out.shape[0] // HEADS // 4

    def kernel(spot, a, b, *outs):
        for k, out in enumerate(outs):

            @pl.when(pl.program_id(0) == k)
            def _(out=out):
                out[:tall, :] = a[...]
                out[tall:, :] = b[...]

    def block(deep):
        return pl.BlockSpec(
            (deep, cols), lambda k, spot: (4 * member_at(spot, k) + 2 * spot[0] + spot[1], 0)
        )

    return call(
        kernel,
        (HEADS,),
        [block(tall), block(low)],
        [whole((tall + low, cols))] * HEADS,
        [((tall + low, cols), w_fc2.dtype)] * HEADS,
        scalars=(spot,),
        args=(w_fc2, w_out),
    )


def stack_members(pieces, spot):
    shape = pieces[0].shape

    def kernel(spot, *refs):
        for k, ref in enumerate(refs[:-1]):
            refs[-1][member_at(spot, k, -1)] = ref[...]

    return call(
        kernel,
        (1,),
        [whole(shape)] * HEADS,
        [whole((HEADS, *shape))],
        [((HEADS, *shape), pieces[0].dtype)],
        scalars=(spot,),
        args=pieces,
    )[0]


def to_members(pieces):
    ring = lax.axis_size(CTX)
    came = [pieces[0]]
    for k in range(1, len(pieces)):
        route = [
            (2 * z + y, (z + k // 2) % ring * 2 + (y ^ (k % 2))) for z in range(ring) for y in range(2)
        ]
        came.append(lax.ppermute(pieces[k], GROUP, route))
    return came


def fold_slots(kept, arrived, slots):
    deep, width = kept.shape
    cols = width // slots

    def kernel(a, b, *outs):
        for s, out in enumerate(outs):
            here = slice(s * cols, (s + 1) * cols)
            out[...] = (a[:, here] + b[:, here].astype(jnp.float32)).astype(jnp.bfloat16)

    return call(
        kernel,
        (1,),
        [whole(kept.shape)] * 2,
        [whole((deep, cols))] * slots,
        [((deep, cols), jnp.bfloat16)] * slots,
        args=(kept, arrived),
    )


def sum_side(mine, came, spot):
    ring, total = mine.shape

    def kernel(spot, a, b, *refs):
        refs[-1][...] = a[...] + b[...]
        for r, out in enumerate(refs[:-1]):
            out[...] = refs[-1][pl.ds((spot[4] + r) % ring, 1), :]

    return call(
        kernel,
        (1,),
        [whole(mine.shape)] * 2,
        [whole((1, total))] * ring,
        [((1, total), jnp.float32)] * ring,
        [pltpu.VMEM((ring, total), jnp.float32)],
        scalars=(spot,),
        args=(mine, came),
    )


def sum_vectors(mine, sent, spot):
    came = rotated(sent, FSDP, 1)
    total, *rows = sum_side(mine, came, spot)
    for r, row in enumerate(rows, 1):
        total = total + rotated(row, CTX, r)
    total = total + rotated(total, CORE, 1)
    return (total + rotated(total, X, 1))[0]


def spread_columns(pieces, meta):
    deep, wide = pieces[0].shape

    def kernel(meta, p0, p1, p2, p3, out):
        for d, p in enumerate((p0, p1, p2, p3)):

            @pl.when(pl.program_id(0) == d)
            def _(p=p):
                out[...] = p[...].astype(jnp.float32)

    return call(
        kernel,
        (4,),
        [whole((deep, wide))] * 4,
        [pl.BlockSpec((deep, wide), lambda d, meta: (meta[0] ^ d, 0))],
        [((4 * deep, wide), jnp.float32)],
        scalars=(meta,),
        args=pieces,
    )[0]


def spread_rows(pieces, meta):
    members, deep, cols = pieces[0].shape
    low = HEAD // 4
    tall = deep - low

    def kernel(meta, p0, p1, p2, p3, fc2, out):
        for d, p in enumerate((p0, p1, p2, p3)):

            @pl.when(pl.program_id(0) == d)
            def _(p=p):
                for m in range(members):
                    fc2[m, 0] = p[m, :tall, :].astype(jnp.float32)
                    out[m, 0] = p[m, tall:, :].astype(jnp.float32)

    fc2, out = call(
        kernel,
        (4,),
        [whole(pieces[0].shape)] * 4,
        [
            pl.BlockSpec((members, 1, tall, cols), lambda d, meta: (0, meta[0] ^ d, 0, 0)),
            pl.BlockSpec((members, 1, low, cols), lambda d, meta: (0, meta[0] ^ d, 0, 0)),
        ],
        [((members, 4, tall, cols), jnp.float32), ((members, 4, low, cols), jnp.float32)],
        scalars=(meta,),
        args=pieces,
    )
    return fc2.reshape(-1, cols), out.reshape(-1, cols)


def spread_halves(own, twin, spot):
    deep, wide = own[0].shape
    steps = 2

    def kernel(spot, a, b, c, d, out):
        @pl.when(pl.program_id(0) == 0)
        def _():
            out[...] = a[...].astype(jnp.float32) + b[...].astype(jnp.float32)

        @pl.when(pl.program_id(0) == 1)
        def _():
            out[...] = c[...].astype(jnp.float32) + d[...].astype(jnp.float32)

    block = (deep // steps, wide)
    mine = pl.BlockSpec(block, lambda h, j, _: (jnp.where(h == 0, j, steps - 1), 0))
    theirs = pl.BlockSpec(block, lambda h, j, _: (jnp.where(h == 0, 0, j), 0))
    return call(
        kernel,
        (2, steps),
        [mine, mine, theirs, theirs],
        [pl.BlockSpec(block, lambda h, j, spot: ((spot[1] ^ h) * steps + j, 0))],
        [((2 * deep, wide), jnp.float32)],
        scalars=(spot,),
        args=(*own, *twin),
    )[0]


def tensor_layer(*args):
    return group_layer(*args)


def group_layer(
    hidden,
    cotangent,
    ln1_gain,
    ln1_bias,
    ln2_gain,
    ln2_bias,
    w_qkv,
    b_qkv,
    w_out,
    b_out,
    w_fc1,
    b_fc1,
    w_fc2,
    b_fc2,
):
    f32, bf16 = jnp.float32, jnp.bfloat16
    ring = lax.axis_size(CTX)
    members = ring * lax.axis_size(FSDP)
    ctx_at, side = lax.axis_index(CTX), lax.axis_index(FSDP)
    x_at, core_at = lax.axis_index(X), lax.axis_index(CORE)
    place, replica = lax.axis_index(GROUP), lax.axis_index(REPLICAS)
    inputs, upstream_own = hidden[0], cotangent[0]
    row_count, width = inputs.shape
    length = ring * row_count
    cols = width // members
    slots = w_qkv.shape[1] // HEAD

    def quarter(array, dim):
        size = array.shape[dim] // 4
        return lax.dynamic_slice_in_dim(array, replica * size, size, dim)

    hid = gather_line(inputs)
    hid_other = gather_side(hid)
    cot = gather_line(upstream_own)
    cot_other = gather_side(cot)

    kind_of = [[0] * slots for _ in range(members)]
    for block in range(slots * members):
        kind_of[block % members][block % slots] = block // HEADS
    kinds = jnp.asarray(kind_of, jnp.int32)[place]
    meta = jnp.concatenate([replica[None], kinds]).astype(jnp.int32)
    spot = jnp.stack([x_at, core_at, place, side, ctx_at, jnp.int32(4)]).astype(jnp.int32)
    token_pos = (
        ((ctx_at - jnp.arange(ring)) % ring)[:, None] * row_count + jnp.arange(row_count)[None]
    ).reshape(length)
    cosine, sine_table = (t[:, 0] for t in rotary_tables(token_pos.astype(f32), ROT))
    rest = ((0, 0), (0, ROPE_LANES - ROT))
    tables = (
        jnp.pad(jnp.concatenate([cosine, cosine], axis=1), rest, constant_values=1.0),
        jnp.pad(jnp.concatenate([-sine_table, sine_table], axis=1), rest),
    )
    b_fc1 = b_fc1.astype(f32)[None]
    twin_core, own_core = (1 - core_at)[None], core_at[None]
    vector = (ln1_gain, ln1_bias, ln2_gain, ln2_bias, b_out, b_fc2, b_qkv)
    vector, meta, spot, tables, b_fc1, twin_core, own_core = lax.optimization_barrier(
        (vector, meta, spot, tables, b_fc1, twin_core, own_core)
    )
    vector = pack_columns([v[None] for v in vector])[0]
    vectors = [vector]
    for r in range(1, ring):
        vectors.append(rotated(vector, CTX, r))
    vectors = jnp.stack(vectors)
    came = rotated(vectors, FSDP, 1)
    both = jnp.stack([vectors, came])
    both = both[jnp.arange(2) ^ side]
    small = jnp.transpose(both[:, (ctx_at - jnp.arange(ring)) % ring], (1, 0, 2))
    small = small.reshape(members, -1).astype(f32)
    gain_one, shift_one, gain_two, shift_two, full_bout, full_bfc2 = (
        small[:, i * cols : (i + 1) * cols].reshape(width) for i in range(6)
    )
    params = jnp.stack([gain_one, shift_one, gain_two, shift_two])
    bias_qkv = small[:, 6 * cols :].reshape(3, HEADS, HEAD)
    bias_qkv = lax.dynamic_slice_in_dim(bias_qkv, place, 1, 1)

    qkv_quarter = quarter(w_qkv, 0)
    moved_columns = []
    for s in range(slots):
        moved_columns.append(
            lax.ppermute(
                qkv_quarter[:, s * HEAD : (s + 1) * HEAD],
                GROUP,
                [(i, (slots * i + s) % members) for i in range(members)],
            )
        )
    moved_columns = pack_columns(moved_columns)

    def replicas(own):
        over_x = rotated(own, X, 1)
        twin = rotated(own, CORE, 1)
        return [own, twin, over_x, rotated(over_x, CORE, 1)]

    head_columns = replicas(moved_columns)
    picked = pick_rows(w_fc2, w_out, spot)
    picked = to_members(picked)
    moved_rows = stack_members(picked, spot)
    row_pieces = replicas(moved_rows)

    rows = (hid, hid_other)
    normed = []
    for i in range(2):
        normed.append(norm_fc1(rows[i], params, w_fc1, b_fc1))
    attn_in, mlp_in, centre, scale, act, slope = zip(*normed)
    head_qkv = join_columns(head_columns, meta)
    first = head_attention(attn_in[0], head_qkv, bias_qkv, tables, spot)
    second = head_attention(attn_in[1], head_qkv, bias_qkv, tables, spot)
    qkv, attended, log_total = zip(first, second)

    def send_places(partial, arrived):
        own, far = fold_blocks(partial, arrived, (0, 2))
        up = lax.ppermute(far, CTX, [(0, 1), (1, 2)])
        down = lax.ppermute(far, CTX, [(2, 1), (3, 2)])
        low, high = fold_blocks(partial, arrived, (1, 3), (down, up))
        low = rotated(low, CTX, -1)
        high = rotated(high, CTX, -3)
        return [own, low, high]

    row_weights, branch_other = project_other(row_pieces, act[1], attended[1], meta)
    out_y = gather_side([branch_other])[0]
    branch = project_own(row_weights, act[0], attended[0])
    out_z = send_places(branch, out_y)

    row_part, row_kept, *upstream = rows_gradient(act, attended, cot + cot_other, spot)
    backs, inner = [None, None], [None, None]
    for i in (1, 0):
        backs[i] = backward(
            upstream[i], row_weights, slope[i], attended[i], qkv[i], log_total[i], tables, spot
        )
        inner[i] = input_side(
            rows[i],
            backs[i][0],
            backs[i][1],
            w_fc1,
            head_qkv,
            centre[i],
            scale[i],
            params,
        )
    d_preact, d_qkv, sum_fc1, sum_qkv, sum_cot = zip(*backs)
    u_y = gather_side(inner[1][1:])[0]
    u_z = send_places(inner[0][1], u_y)

    row_part = rotated(row_part, CORE, 1)
    row_sent, row_keep = rows_gradient(act, None, upstream, spot, (row_part, row_kept))
    row_sent = rotated(row_sent, X, 1)
    col_part = columns_gradient(attn_in, d_qkv, meta, spot)[0]
    col_part = rotated(col_part, CORE, 1)
    col_sent, col_keep = columns_gradient(attn_in, d_qkv, meta, spot, col_part)
    col_sent = rotated(col_sent, X, 1)
    fc1_part = fc1_gradient(mlp_in, d_preact, twin_core)
    fc1_part = rotated(fc1_part, CORE, 1)
    fc1_half = fc1_gradient(mlp_in, d_preact, own_core, fc1_part)
    fc1_sent = rotated(fc1_half, X, 1)
    fc1_twin = rotated(fc1_half, CORE, 1)
    fc1_both = rotated(fc1_sent, CORE, 1)

    vectors = pack_sums((inner[0][0], inner[1][0]), sum_qkv, sum_cot, sum_fc1, spot)
    vectors = sum_vectors(*vectors, spot)
    g1, s1, g2, s2 = (vectors[i * cols : (i + 1) * cols] for i in range(4))
    bqkv_grad, bout_grad, bfc1_grad = jnp.split(
        vectors[4 * cols :], (slots * HEAD, slots * HEAD + cols)
    )

    col_part = fold_slots(col_keep, col_sent, slots)
    col_back = []
    for s in range(slots):
        col_back.append(
            lax.ppermute(
                col_part[s],
                GROUP,
                [((slots * i + s) % members, i) for i in range(members)],
            )
        )
    row_part = fold_rows(row_keep, row_sent, spot)
    row_part = to_members(row_part)
    row_back = stack_members(row_part, spot)
    fc1_grad = spread_halves((fc1_half, fc1_sent), (fc1_twin, fc1_both), spot)
    col_back = pack_columns(col_back)
    col_back = replicas(col_back)
    qkv_grad = spread_columns(col_back, meta)
    row_back = replicas(row_back)
    fc2_grad, out_grad = spread_rows(row_back, meta)

    own_f = inputs.astype(f32)
    branch = sum(v.astype(f32) for v in out_z)
    output = (own_f + (branch + full_bout + full_bfc2)).astype(bf16)
    merged = sum(v.astype(f32) for v in u_z)
    own_normed, own_std = normalize(own_f)
    input_grad = (
        upstream_own.astype(f32) + norm_backward(merged, own_normed, own_std)
    ).astype(bf16)

    return (
        output[None],
        input_grad[None],
        g1,
        s1,
        g2,
        s2,
        qkv_grad,
        bqkv_grad,
        out_grad,
        bout_grad,
        fc1_grad,
        bfc1_grad,
        fc2_grad,
        bout_grad,
    )


def solution(mesh):
    sizes = dict(mesh.shape)
    fits = (sizes[CTX], sizes[FSDP], sizes[DP]) == (HEADS // 2, 2, 4)
    if fits:
        mesh = Mesh(
            mesh.devices.reshape(2, 2, sizes[CTX], sizes[FSDP]),
            (X, CORE, CTX, FSDP),
        )
    rows = P((*(REPLICAS if fits else (DP,)), FSDP), CTX, None)
    vector, matrix = P(GROUP), P(None, GROUP)
    params = (vector,) * 4 + (matrix, vector) * 4
    return jax.shard_map(
        tensor_layer if fits else plain_layer,
        mesh=mesh,
        in_specs=(rows, rows, *params),
        out_specs=(rows, rows, *params),
        check_vma=False,
    )
```
